32 devices in a mesh: tis: 16 (over z, y, core), ves: 2 (over x).
Axes of the slice: x: 2, y: 2, z: 4, core: 2. Of those that a mesh axis runs over, the one named last changes fastest.
Arguments:
- point_xyz: float32 [3, 65536], P(None, 'tis'), may hold values from 0 to 1
- point_cell: int32 [65536], P('tis'), may hold values from 0 to 63, never falling along the last dimension, each value on 1 to 4096 neighbouring positions
- seg_xyz: float32 [3, 8192], P(None, 'ves'), may hold values from 0 to 1
- seg_radius: float32 [8192], P('ves'), may hold values from 0.004 to 0.02
- conductance: float32 [8192], P('ves'), may hold values from 0.5 to 2
- flow_inv: float32 [8192], P('ves'), may hold values from 0.1 to 0.5
- parent: int32 [8192], P('ves'), may hold values from 0 to 8191, as said below
- inflow: float32 [8, 8192], P(None, 'ves'), may hold values from 2 to 4
- rate_table: float32 [8, 64], replicated, may hold values from 0.5 to 2
- half_sat: float32 [8], replicated, may hold values from 0.3 to 1
- diffusivity: float32 [8], replicated, may hold values from 0.5 to 2
- base_level: float32 [8], replicated, may hold values from -0.5 to 0.5
- sources: float32 [8, 8192], P(None, 'ves'), may hold values from 0.5 to 2
- contents: float32 [8, 8192], P(None, 'ves'), may hold values from 1 to 3
Outputs:
- tissue_level: float32 [8, 65536], P(None, 'tis')
- seg_sources: float32 [8, 8192], P(None, 'ves')
- blood_content: float32 [8, 8192], P(None, 'ves')
The draws below stay inside these ranges and needn't reach their ends.
Inputs may be any that keep to these rules, and one draw needn't show every extreme that they name: Each segment is a root (parent equals its own index) or its parent lies among the 4096 segments before it: j - 4096 <= parent[j] < j. Points are ordered by region: point_cell never falls along the points.
All inputs are finite; a program needn't handle non-finite values.
Results may differ from the reference program's by a relative error of at most 0.0003.
Values sent between devices are 32-bit elements; how exact they have to be, the bound alone decides.
No kernel may reach another device: no remote copies, remote signals or barrier semaphores. Data moves between devices by JAX's collectives and lax.ppermute only.
A program may use at most 128 MiB of HBM per device.

```python
import math
import jax
import jax.numpy as jnp
import numpy as np
from jax import lax

SOL = 8
PT_DEV = 4096
SEG_DEV = 4096
ITERS = 3
CELLS = 64
NP = 65536
NS = 8192
N_TIS = 16


path_count = 4


def vessel_midpoints(key, reach, wiggle):
    base = jax.random.fold_in(key, 23)
    keys = jax.random.split(base, 6)
    start = jax.random.uniform(keys[0], (3, path_count), minval=0.0, maxval=1.0)
    heading = jax.random.uniform(keys[1], (3, path_count), minval=-1.0, maxval=1.0)
    heading = heading / jnp.sqrt(jnp.sum(heading * heading, axis=0, keepdims=True) + 0.05)
    amplitude = wiggle * jax.random.uniform(keys[2], (3, path_count, 3), minval=0.5, maxval=1.5)
    phase = jax.random.uniform(keys[3], (3, path_count, 3), minval=0.0, maxval=2.0 * math.pi)
    which = jax.random.randint(keys[4], (NS,), 0, path_count)
    along = jax.random.uniform(keys[5], (NS,), minval=0.0, maxval=1.0)
    harmonic = jnp.arange(1, 4, dtype=jnp.float32)
    raw = start[:, which] + reach * along[None, :] * heading[:, which]
    wave = amplitude[:, which, :] * jnp.sin(2.0 * math.pi * harmonic[None, None, :] * along[None, :, None] + phase[:, which, :])
    raw = raw + jnp.sum(wave, axis=2)
    return (1.0 - jnp.abs(jnp.mod(raw, 2.0) - 1.0)).astype(jnp.float32)


def draw_seg_xyz(key, part):
    reach, wiggle = (1.5, 0.02)
    return vessel_midpoints(key, reach, wiggle)


def draw_point_xyz(key, part):
    reach, wiggle = (1.5, 0.02)
    midpoints = vessel_midpoints(key, reach, wiggle)
    keys = jax.random.split(jax.random.fold_in(key, 29), 5)
    picked = jax.random.randint(keys[0], (NP,), 0, NS)
    offset = jnp.exp(jax.random.uniform(keys[1], (NP,), minval=math.log(0.06), maxval=math.log(0.3)))
    near_share = 0.95
    direction = jax.random.normal(keys[2], (3, NP))
    direction = direction / jnp.sqrt(jnp.sum(direction * direction, axis=0, keepdims=True) + 0.001)
    nearby = midpoints[:, picked] + offset[None, :] * direction
    faraway = jax.random.uniform(keys[3], (3, NP), minval=0.0, maxval=1.0)
    mixing = jax.random.uniform(keys[4], (NP,), minval=0.0, maxval=1.0) < near_share
    placed = jnp.where(mixing[None, :], nearby, faraway)
    return jnp.clip(placed, 0.0, 1.0).astype(jnp.float32)


def draw_parent(key, part):
    first_key, second_key = jax.random.split(jax.random.fold_in(key, 11))
    seg_index = jnp.arange(NS, dtype=jnp.int32)
    distance = jax.random.randint(first_key, (NS,), 1, SEG_DEV + 1)
    root_pick = jax.random.randint(second_key, (NS,), 0, 8)
    candidate = seg_index - distance
    return jnp.where((root_pick == 0) | (candidate < 0), seg_index, candidate).astype(jnp.int32)


def block_levels(stream_key, dims, pieces, smallest, high):
    loudness = 1.0
    for position, shards_of in pieces:
        steps = jax.random.uniform(jax.random.fold_in(jax.random.fold_in(stream_key, 6), position), (shards_of,), jnp.float32, smallest / len(pieces), high / len(pieces))
        loudness = loudness * jnp.repeat(jnp.exp(steps), dims[position] // shards_of).reshape((-1,) + (1,) * (len(dims) - 1 - position))
    return loudness


def split_up(amount, total, most, slope):
    loads = [(1 << 20) // math.isqrt(rank ** slope) + 1 for rank in range(2, amount + 1)]
    surplus, holding = total - most - (amount - 1), [1] * (amount - 1)
    while surplus > 0:
        candidates = [i for i in range(amount - 1) if holding[i] < most]
        whole, left = sum([loads[i] for i in candidates]), surplus
        for i in candidates:
            extra = min(most - holding[i], max(1, left * loads[i] // whole), surplus)
            holding[i] = holding[i] + extra
            surplus = surplus - extra
    return np.array([most] + holding)


def uneven(stream_key, count, total, limit, slope):
    if count == 2:
        one = jax.random.randint(stream_key, (), max(1, total - limit), min(limit, total - 1) + 1)
        return jnp.stack([one, total - one])
    lengths = jnp.asarray(split_up(count, total, limit, slope), jnp.int32)
    couples = (count - 1) // 2
    giver, receiver = lengths[1:1 + 2 * couples:2], lengths[2:2 + 2 * couples:2]
    slack = jnp.minimum(giver - 1, limit - receiver)
    moved = jax.random.randint(jax.random.fold_in(stream_key, 1), (couples,), 0, 1 << 20) % (slack + 1)
    lengths = lengths.at[1:1 + 2 * couples:2].set(giver - moved).at[2:2 + 2 * couples:2].set(receiver + moved)
    return lengths[jax.random.permutation(jax.random.fold_in(stream_key, 2), count)]


def setup_inputs(seed: int = 0) -> dict:
    arg_keys = jax.random.split(jax.random.key(seed), 15)
    return {
        "point_xyz": draw_point_xyz(jax.random.fold_in(arg_keys[14], 71), 0),
        "point_cell": jnp.searchsorted(jnp.cumsum(uneven(arg_keys[1], CELLS, NP, PT_DEV, 1)), jnp.arange(NP), side="right").astype(jnp.int32),
        "seg_xyz": draw_seg_xyz(jax.random.fold_in(arg_keys[14], 71), 0),
        "seg_radius": jnp.clip(jnp.exp(math.log(0.02) - 1.6094378 * jax.random.uniform(arg_keys[3], (NS,), jnp.float32) ** block_levels(arg_keys[3], (NS,), ((0, 2),), -0.2, 0.2)), 0.004, 0.02),
        "conductance": jnp.clip(jnp.exp(math.log(2.0) - 1.3862944 * jax.random.uniform(arg_keys[4], (NS,), jnp.float32) ** block_levels(arg_keys[4], (NS,), ((0, 2),), -0.2, 0.2)), 0.5, 2.0),
        "flow_inv": jnp.clip(jnp.exp(math.log(0.5) - 1.609438 * jax.random.uniform(arg_keys[5], (NS,), jnp.float32) ** block_levels(arg_keys[5], (NS,), ((0, 2),), -0.2, 0.2)), 0.1, 0.5),
        "parent": draw_parent(jax.random.fold_in(arg_keys[14], 71), 0),
        "inflow": jnp.clip(2.0 + 2.0 * jax.random.uniform(arg_keys[7], (SOL, NS), jnp.float32) ** block_levels(arg_keys[7], (SOL, NS), ((1, 2),), -0.2, 0.2), 2.0, 4.0),
        "rate_table": jnp.clip(jnp.exp(jax.random.uniform(arg_keys[8], (SOL, CELLS), jnp.float32, math.log(0.5), math.log(2.0))), 0.5, 2.0),
        "half_sat": jnp.clip(jnp.exp(jax.random.uniform(arg_keys[9], (SOL,), jnp.float32, math.log(0.3), math.log(1.0))), 0.3, 1.0),
        "diffusivity": jnp.clip(jnp.exp(jax.random.uniform(arg_keys[10], (SOL,), jnp.float32, math.log(0.5), math.log(2.0))), 0.5, 2.0),
        "base_level": jnp.clip(jax.random.uniform(arg_keys[11], (SOL,), jnp.float32, -0.5, 0.5), -0.5, 0.5),
        "sources": jnp.clip(0.5 + 1.5 * jax.random.uniform(arg_keys[12], (SOL, NS), jnp.float32) ** block_levels(arg_keys[12], (SOL, NS), ((1, 2),), -0.2, 0.2), 0.5, 2.0),
        "contents": jnp.clip(1.0 + 2.0 * jax.random.uniform(arg_keys[13], (SOL, NS), jnp.float32) ** block_levels(arg_keys[13], (SOL, NS), ((1, 2),), -0.2, 0.2), 1.0, 3.0),
    }


RELAX = 0.5
BALANCE = 0.5

def kernel_rows(points, seg_pos, radius):
    dist_sq = (points[0][:, None] - seg_pos[0][None, :]) ** 2
    dist_sq = dist_sq + (points[1][:, None] - seg_pos[1][None, :]) ** 2
    dist_sq = dist_sq + (points[2][:, None] - seg_pos[2][None, :]) ** 2
    return lax.rsqrt(dist_sq + (radius * radius)[None, :]).astype(jnp.bfloat16)

def reference(point_xyz, point_cell, seg_xyz, seg_radius, conductance, flow_inv, parent, inflow, rate_table, half_sat, diffusivity, base_level, sources, contents):
    rates = jnp.take(rate_table, point_cell, axis=1)
    point_blocks = point_xyz.reshape(3, N_TIS, PT_DEV).transpose(1, 0, 2)
    rate_blocks = rates.reshape(SOL, N_TIS, PT_DEV).transpose(1, 0, 2)
    seg_index = jnp.arange(NS, dtype=jnp.int32)
    tissue_level = jnp.zeros((SOL, NP), jnp.float32)
    for sweep in range(ITERS):
        src_bf = sources.astype(jnp.bfloat16)

        def one_block(totals, inputs):
            pts_block, rate_block = inputs
            kernel_tile = kernel_rows(pts_block, seg_xyz, seg_radius)
            raw_sum = lax.dot_general(src_bf, kernel_tile, (((1,), (1,)), ((), ())), preferred_element_type=jnp.float32)
            level = base_level[:, None] + raw_sum / (diffusivity[:, None] * NS)
            sink_field = rate_block * level / (jnp.abs(level) + half_sat[:, None])
            wall_acc = totals[0] + jnp.dot(sink_field.astype(jnp.bfloat16), kernel_tile, preferred_element_type=jnp.float32)
            return ((wall_acc, totals[1] + lax.optimization_barrier(jnp.sum(sink_field, axis=1))), level)
        init = (jnp.zeros((SOL, NS), jnp.float32), jnp.zeros((SOL,), jnp.float32))
        (wall_raw, sink_total), levels = lax.scan(one_block, init, (point_blocks, rate_blocks))
        tissue_level = levels.transpose(1, 0, 2).reshape(SOL, NP)
        source_total = lax.optimization_barrier(jnp.sum(sources, axis=1))
        outflow = contents - sources * flow_inv[None, :]
        contents = jnp.where((parent == seg_index)[None, :], inflow, jnp.take(outflow, parent, axis=1))
        wall_field = wall_raw / (diffusivity[:, None] * NP)
        sources = RELAX * sources + RELAX * conductance[None, :] * (contents - wall_field)
        base_level = base_level + BALANCE * (source_total / NS - sink_total / NP)
    return (tissue_level, sources, contents)
```

```python
import functools

import jax
import jax.numpy as jnp
from jax import lax
from jax.experimental import pallas as pl
from jax.experimental.pallas import tpu as pltpu
from jax.sharding import PartitionSpec as P

ITERS = 3

RELAX = 0.5
BALANCE = 0.5
LANES = 128
PARTS = 2


VM = pl.BlockSpec(memory_space=pltpu.VMEM)
SM = pl.BlockSpec(memory_space=pltpu.SMEM)
F32 = jnp.float32
BF16 = jnp.bfloat16


def call(kernel, outs, ins, name, scratch=(), limit=20, flops=0, bytes_accessed=0):
    specs = [SM if space == "s" else VM for space, _ in ins]
    arrays = [
        pltpu.with_memory_space_constraint(value, pltpu.VMEM) if space == "k" else value
        for space, value in ins
    ]
    return pl.pallas_call(
        kernel,
        out_shape=tuple(outs),
        in_specs=specs,
        out_specs=(VM,) * len(outs),
        scratch_shapes=list(scratch),
        compiler_params=pltpu.CompilerParams(vmem_limit_bytes=limit << 20),
        cost_estimate=pl.CostEstimate(
            flops=flops, bytes_accessed=bytes_accessed, transcendentals=0
        ),
        name=name,
    )(*arrays)


def shape(*dims):
    return jax.ShapeDtypeStruct(dims, F32)


def at(block, size):
    return pl.ds(pl.multiple_of(block * size, size), size)


def lane_sum(ref, solutes, cols):
    acc = ref[:, 0:LANES]
    for tile in range(1, cols // LANES):
        acc = acc + ref[:, tile * LANES : (tile + 1) * LANES]
    return jnp.broadcast_to(jnp.sum(acc, axis=1, keepdims=True), (solutes, LANES))


def prep_kernel(
    total_pts, total_segs, table_ref, cell_ref, hs_ref, diff_ref, base_ref, src_ref, cont_ref,
    flow_ref, rates_ref, par_ref, base_out, out_ref
):
    solutes, pts = rates_ref.shape
    row = lax.broadcasted_iota(jnp.int32, (solutes, LANES), 0)

    def spread(ref):
        acc = jnp.full((solutes, LANES), ref[0], F32)
        for s in range(1, solutes):
            acc = jnp.where(row == s, ref[s], acc)
        return acc

    diff = spread(diff_ref)
    par_ref[0] = spread(hs_ref)
    par_ref[1] = diff * total_segs
    par_ref[2] = diff * total_pts
    base_out[...] = spread(base_ref)
    out_ref[...] = cont_ref[...] - src_ref[...] * flow_ref[...]
    tiles = table_ref.shape[1] // LANES
    for p in range(pts // LANES):
        cols = slice(p * LANES, (p + 1) * LANES)
        cell = jnp.broadcast_to(cell_ref[0:1, cols], (solutes, LANES))
        lane = lax.bitwise_and(cell, LANES - 1)
        acc = jnp.take_along_axis(table_ref[:, 0:LANES], lane, axis=1)
        for t in range(1, tiles):
            got = jnp.take_along_axis(table_ref[:, t * LANES : (t + 1) * LANES], lane, axis=1)
            acc = jnp.where(lax.shift_right_logical(cell, 7) == t, got, acc)
        rates_ref[:, cols] = acc


def build_kernel(part, pts_ref, seg_ref, rad_ref, src_ref, k_ref, t_ref, pb, rr, sb):
    rows, cols = k_ref.shape
    solutes = src_ref.shape[0]
    rb = min(256, rows)
    pc = min(512, cols)
    rg = 16
    rr[...] = rad_ref[...] * rad_ref[...]
    sb[...] = src_ref[...].astype(BF16)

    def load_points(r):
        p = pts_ref[:, pl.ds(pl.multiple_of(part * rows + r * rb, rb), rb)]
        p = jnp.concatenate([p, jnp.zeros((5, rb), F32)], axis=0)
        pt = jnp.transpose(p)
        for q in range(3):
            pb[q] = jnp.broadcast_to(pt[:, q : q + 1], (rb, LANES))

    def make(r, c):
        for g in range(rb // rg):
            where = pl.ds(pl.multiple_of(r * rb + g * rg, rg), rg)
            px, py, pz = (pb[q, g * rg : (g + 1) * rg, :] for q in range(3))
            for t in range(0, pc // LANES, 2):
                first = c * pc + t * LANES
                pair = []
                for u in (0, 1):
                    at_cols = slice(first + u * LANES, first + (u + 1) * LANES)
                    dx = px - seg_ref[0:1, at_cols]
                    dy = py - seg_ref[1:2, at_cols]
                    dz = pz - seg_ref[2:3, at_cols]
                    pair.append(lax.rsqrt(((dx * dx + dy * dy) + dz * dz) + rr[:, at_cols]))
                k_ref[where, first : first + 2 * LANES] = jnp.concatenate(pair, axis=1).astype(BF16)

    def multiply(r, c):
        piece = slice(c * pc, (c + 1) * pc)
        return lax.dot_general(
            sb[:, piece], k_ref[at(r, rb), piece], (((1,), (1,)), ((), ())),
            preferred_element_type=F32,
        )

    n_pc = cols // pc
    load_points(0)
    for c in range(n_pc):
        make(0, c)

    def body(r, carry):
        load_points(r)
        acc = None
        for c in range(n_pc):
            got = multiply(r - 1, c)
            acc = got if acc is None else acc + got
            make(r, c)
        t_ref[:, at(r - 1, rb)] = acc
        return carry

    lax.fori_loop(1, rows // rb, body, 0)
    acc = None
    for c in range(n_pc):
        got = multiply(rows // rb - 1, c)
        acc = got if acc is None else acc + got
    t_ref[:, rows - rb : rows] = acc
    if part == 0:
        t_ref[:, rows : rows + LANES] = lane_sum(src_ref, solutes, cols)


def tissue_kernel(k_ref, src_ref, t_ref, sb, *, part):
    rows, cols = k_ref.shape
    solutes = src_ref.shape[0]
    sb[...] = src_ref[...].astype(BF16)
    rb = min(1024, rows)
    pc = min(1024, cols)

    def body(r, carry):
        acc = None
        for c in range(cols // pc):
            piece = slice(c * pc, (c + 1) * pc)
            got = lax.dot_general(
                sb[:, piece], k_ref[at(r, rb), piece], (((1,), (1,)), ((), ())),
                preferred_element_type=F32,
            )
            acc = got if acc is None else acc + got
        t_ref[:, at(r, rb)] = acc
        return carry

    lax.fori_loop(0, rows // rb, body, 0)
    if part == 0:
        t_ref[:, rows : rows + LANES] = lane_sum(src_ref, solutes, cols)


def join_kernel(core_ref, mine_ref, theirs_ref, cont_ref, flow_ref, src_ref, out_ref):
    half = mine_ref.shape[1]
    core = core_ref[0]
    src_ref[:, at(core, half)] = mine_ref[...]
    src_ref[:, at(1 - core, half)] = theirs_ref[...]
    out_ref[...] = cont_ref[...] - src_ref[...] * flow_ref[...]


def wall_kernel(part, last, *refs):
    if part == 0:
        k_ref, own_ref, got_ref, rates_ref, par_ref, base_ref, wall_ref, level_ref, tmp = refs
    else:
        (
            k_ref, own_ref, got_ref, rates_ref, par_ref, base_ref, core_ref, before_ref, level_in,
            keep_ref, send_ref, *more, tmp, wall_scr,
        ) = refs
        level_ref = more[0] if last else None
        wall_ref = wall_scr
    rows, cols = k_ref.shape
    solutes = rates_ref.shape[0]
    hs, dn, base = par_ref[0], par_ref[1], base_ref[...]
    total = jnp.zeros((solutes, LANES), F32)
    for p in range(rows // LANES):
        here = slice(p * LANES, (p + 1) * LANES)
        level = base + (own_ref[:, here] + got_ref[:, here]) / dn
        rate = rates_ref[:, part * rows + p * LANES : part * rows + (p + 1) * LANES]
        sink = rate * level / (jnp.abs(level) + hs)
        total = total + sink
        tmp[:, here] = sink.astype(BF16)
        if part == 0:
            level_ref[:, here] = level
        elif last:
            level_ref[:, rows + p * LANES : rows + (p + 1) * LANES] = level
    if part != 0 and last:
        level_ref[:, 0:rows] = level_in[...]
    total = jnp.broadcast_to(jnp.sum(total, axis=1, keepdims=True), (solutes, LANES))
    rb = min(256, rows)

    def body(r, carry):
        wall_ref[:, 0:cols] += jnp.dot(
            tmp[:, at(r, rb)], k_ref[at(r, rb), :], preferred_element_type=F32
        )
        return carry

    if part == 0:
        wall_ref[:, 0:cols] = jnp.zeros((solutes, cols), F32)
        wall_ref[:, cols : cols + LANES] = total
    else:
        wall_ref[:, 0:cols] = before_ref[:, 0:cols]
        total = total + before_ref[:, cols : cols + LANES]
    lax.fori_loop(0, rows // rb, body, 0)
    if part != 0:
        half = cols // 2
        core = core_ref[0]
        keep_ref[:, 0:half] = wall_ref[:, at(core, half)]
        send_ref[:, 0:half] = wall_ref[:, at(1 - core, half)]
        keep_ref[:, half : half + LANES] = total
        send_ref[:, half : half + LANES] = total


def gather_kernel(ves_ref, parent_ref, up_ref, out_ref, inflow_ref, cont_ref, joined):
    solutes, cols = out_ref.shape
    joined[:, 0:cols] = up_ref[...]
    joined[:, cols : 2 * cols] = out_ref[...]
    first = ves_ref[0] * cols
    tiles = cols // LANES

    def body(j, carry):
        here = at(j, LANES)
        parent = jnp.broadcast_to(parent_ref[0:1, here], (solutes, LANES))
        seg = first + j * LANES + lax.broadcasted_iota(jnp.int32, (solutes, LANES), 1)
        place = parent - (first - cols)
        lane = lax.bitwise_and(place, LANES - 1)
        tile = lax.shift_right_arithmetic(place, 7) - j
        acc = inflow_ref[:, here]
        tile = jnp.where(parent == seg, -1, tile)
        for t in range(tiles + 1):
            got = jnp.take_along_axis(joined[:, at(j + t, LANES)], lane, axis=1)
            acc = jnp.where(tile == t, got, acc)
        cont_ref[:, here] = acc
        return carry

    lax.fori_loop(0, tiles, body, 0)


def update_kernel(
    total_pts, total_segs, core_ref, a_ref, b_ref, own_ref, got_ref, src_ref, cont_ref, cond_ref,
    par_ref, base_ref, new_ref, base_out
):
    half = new_ref.shape[1]
    rows = own_ref.shape[1] - LANES
    core = core_ref[0]
    dp = par_ref[2]
    for p in range(half // LANES):
        here = slice(p * LANES, (p + 1) * LANES)
        there = at(core * (half // LANES) + p, LANES)
        wall = (a_ref[:, here] + b_ref[:, here]) / dp
        new_ref[:, here] = RELAX * src_ref[:, there] + RELAX * cond_ref[:, there] * (
            cont_ref[:, there] - wall
        )
    sink_total = a_ref[:, half : half + LANES] + b_ref[:, half : half + LANES]
    source_total = own_ref[:, rows : rows + LANES] + got_ref[:, rows : rows + LANES]
    base_out[...] = base_ref[...] + BALANCE * (
        source_total / total_segs - sink_total / total_pts
    )


def body(
    point_xyz,
    point_cell,
    seg_xyz,
    seg_radius,
    conductance,
    flow_inv,
    parent,
    inflow,
    rate_table,
    half_sat,
    diffusivity,
    base_level,
    sources,
    contents,
):
    pts = point_xyz.shape[1]
    cols = seg_xyz.shape[1]
    solutes = sources.shape[0]
    n_tis = lax.axis_size("tis")
    n_ves = lax.axis_size("ves")
    total_pts = pts * n_tis
    total_segs = cols * n_ves
    rows = pts // PARTS
    half = cols // 2
    tis = lax.axis_index("tis")
    core = (tis % 2).astype(jnp.int32).reshape(1)
    ves = lax.axis_index("ves").astype(jnp.int32).reshape(1)

    def swap(value, bit):
        return lax.ppermute(value, "tis", [(i, i ^ bit) for i in range(n_tis)])

    def across(value):
        if n_ves == 2:
            return value, lax.ppermute(value, "ves", [(0, 1), (1, 0)])
        return lax.psum(value, "ves"), jnp.zeros_like(value)

    n_cells = rate_table.shape[1]
    table = jnp.pad(rate_table, ((0, 0), (0, -n_cells % LANES)))
    cond = conductance.reshape(1, cols)
    flow = flow_inv.reshape(1, cols)
    par_row = parent.reshape(1, cols)

    rates, par, base, outflow = call(
        functools.partial(prep_kernel, float(total_pts), float(total_segs)),
        [shape(solutes, pts), shape(3, solutes, LANES), shape(solutes, LANES), shape(solutes, cols)],
        [
            ("v", table), ("v", point_cell.reshape(1, pts)), ("s", half_sat), ("s", diffusivity),
            ("s", base_level), ("v", sources), ("v", contents), ("v", flow),
        ],
        "prep",
    )
    halves = [None, None]
    level = None
    for sweep in range(ITERS):
        last = sweep == ITERS - 1
        upstream = lax.ppermute(outflow, "ves", [(i, i + 1) for i in range(n_ves - 1)])
        own, got = [], []
        for part in range(PARTS):
            width = rows + (LANES if part == 0 else 0)
            if sweep == 0:
                halves[part], t = call(
                    functools.partial(build_kernel, part),
                    [pltpu.VMEM((rows, cols), BF16), shape(solutes, width)],
                    [("v", point_xyz), ("v", seg_xyz), ("v", seg_radius.reshape(1, cols)), ("v", sources)],
                    f"build{part}",
                    scratch=[
                        pltpu.VMEM((3, min(256, rows), LANES), F32), pltpu.VMEM((1, cols), F32),
                        pltpu.VMEM((solutes, cols), BF16),
                    ],
                    limit=24,
                    flops=10 * rows * cols,
                    bytes_accessed=20_000_000,
                )
            else:
                (t,) = call(
                    functools.partial(tissue_kernel, part=part),
                    [shape(solutes, width)],
                    [("k", halves[part]), ("v", sources)],
                    f"tissue{part}",
                    scratch=[pltpu.VMEM((solutes, cols), BF16)],
                    flops=2 * solutes * rows * cols,
                    bytes_accessed=10_000_000,
                )
            t, other = across(t)
            own.append(t)
            got.append(other)
        wall, level = call(
            functools.partial(wall_kernel, 0, last),
            [shape(solutes, cols + LANES), shape(solutes, rows)],
            [("k", halves[0]), ("v", own[0]), ("v", got[0]), ("v", rates), ("v", par), ("v", base)],
            "wall0",
            scratch=[pltpu.VMEM((solutes, rows), BF16)],
            flops=2 * solutes * rows * cols,
            bytes_accessed=10_000_000,
        )
        keep, send, *more = call(
            functools.partial(wall_kernel, 1, last),
            [shape(solutes, half + LANES)] * 2 + ([shape(solutes, pts)] if last else []),
            [
                ("k", halves[1]), ("v", own[1]), ("v", got[1]), ("v", rates), ("v", par),
                ("v", base), ("s", core), ("v", wall), ("v", level),
            ],
            "wall1",
            scratch=[pltpu.VMEM((solutes, rows), BF16), pltpu.VMEM((solutes, cols), F32)],
            flops=2 * solutes * rows * cols,
            bytes_accessed=10_000_000,
        )
        if last:
            level = more[0]
        (new_contents,) = call(
            gather_kernel,
            [shape(solutes, cols)],
            [("s", ves), ("v", par_row), ("v", upstream), ("v", outflow), ("v", inflow)],
            "gather",
            scratch=[pltpu.VMEM((solutes, 2 * cols), F32)],
            flops=solutes * cols * 33,
            bytes_accessed=8_000_000,
        )
        theirs = swap(send, 1)
        bit = 2
        while bit < n_tis:
            keep = keep + theirs
            theirs = swap(keep, bit)
            bit *= 2
        new, base = call(
            functools.partial(update_kernel, float(total_pts), float(total_segs)),
            [shape(solutes, half), shape(solutes, LANES)],
            [
                ("s", core), ("v", keep), ("v", theirs), ("v", own[0]), ("v", got[0]),
                ("v", sources), ("v", new_contents), ("v", cond), ("v", par), ("v", base),
            ],
            "update",
        )
        contents = new_contents
        sources, outflow = call(
            join_kernel,
            [shape(solutes, cols)] * 2,
            [("s", core), ("v", new), ("v", swap(new, 1)), ("v", contents), ("v", flow)],
            "join",
        )
    return (level, sources, contents)


def solution(mesh):
    return jax.shard_map(
        body,
        mesh=mesh,
        in_specs=(
            P(None, "tis"),
            P("tis"),
            P(None, "ves"),
            P("ves"),
            P("ves"),
            P("ves"),
            P("ves"),
            P(None, "ves"),
            P(),
            P(),
            P(),
            P(),
            P(None, "ves"),
            P(None, "ves"),
        ),
        out_specs=(P(None, "tis"), P(None, "ves"), P(None, "ves")),
        check_vma=False,
    )
```

```python
import functools

import jax
import jax.numpy as jnp
from jax import lax
from jax.experimental import pallas as pl
from jax.experimental.pallas import tpu as pltpu
from jax.sharding import PartitionSpec as P

ITERS = 3

RELAX = 0.5
BALANCE = 0.5
LANES = 128
PARTS = 2
CHUNKS = 2
BUILD_ROWS = 128
BUILD_LIMIT = 12


VM = pl.BlockSpec(memory_space=pltpu.VMEM)
SM = pl.BlockSpec(memory_space=pltpu.SMEM)
F32 = jnp.float32
BF16 = jnp.bfloat16


def call(kernel, outs, ins, name, scratch=(), limit=4, flops=0, bytes_accessed=0):
    specs = [SM if space in ("s", "hs") else VM for space, _ in ins]
    pinned = {"k": pltpu.VMEM, "h": pltpu.HBM, "hs": pltpu.HBM}
    arrays = [
        pltpu.with_memory_space_constraint(value, pinned[space]) if space in pinned else value
        for space, value in ins
    ]
    return pl.pallas_call(
        kernel,
        out_shape=tuple(outs),
        in_specs=specs,
        out_specs=(VM,) * len(outs),
        scratch_shapes=list(scratch),
        compiler_params=pltpu.CompilerParams(vmem_limit_bytes=limit << 20),
        cost_estimate=pl.CostEstimate(
            flops=flops, bytes_accessed=bytes_accessed, transcendentals=0
        ),
        name=name,
    )(*arrays)


def shape(*dims):
    return jax.ShapeDtypeStruct(dims, F32)


def at(block, size):
    return pl.ds(pl.multiple_of(block * size, size), size)


def lane_sum(ref, solutes, cols):
    acc = ref[:, 0:LANES]
    for tile in range(1, cols // LANES):
        acc = acc + ref[:, tile * LANES : (tile + 1) * LANES]
    return jnp.broadcast_to(jnp.sum(acc, axis=1, keepdims=True), (solutes, LANES))


def prepare(
    total_pts, total_segs, table_ref, cell_ref, hs_ref, diff_ref, base_ref, cont_ref, flow_ref,
    src_ref, rates_ref, par_ref, base_out, out_ref
):
    solutes, pts = rates_ref.shape
    row = lax.broadcasted_iota(jnp.int32, (solutes, LANES), 0)

    def spread(ref):
        acc = jnp.full((solutes, LANES), ref[0], F32)
        for s in range(1, solutes):
            acc = jnp.where(row == s, ref[s], acc)
        return acc

    diff = spread(diff_ref)
    par_ref[0] = spread(hs_ref)
    par_ref[1] = diff * total_segs
    par_ref[2] = diff * total_pts
    base_out[...] = spread(base_ref)
    out_ref[...] = cont_ref[...] - src_ref[...] * flow_ref[...]
    n_cells = table_ref.shape[1]
    tiles = pl.cdiv(n_cells, LANES)
    spare = tiles * LANES - n_cells
    table = table_ref[...]
    if spare:
        table = jnp.concatenate([table, jnp.zeros((solutes, spare), F32)], axis=1)
    for p in range(pts // LANES):
        cols = slice(p * LANES, (p + 1) * LANES)
        cell = jnp.broadcast_to(cell_ref[0:1, cols], (solutes, LANES))
        lane = lax.bitwise_and(cell, LANES - 1)
        acc = jnp.take_along_axis(table[:, 0:LANES], lane, axis=1)
        for t in range(1, tiles):
            got = jnp.take_along_axis(table[:, t * LANES : (t + 1) * LANES], lane, axis=1)
            acc = jnp.where(lax.shift_right_logical(cell, 7) == t, got, acc)
        rates_ref[:, cols] = acc


def build_kernel(part, total_pts, total_segs, *refs):
    if part == 0:
        core_ref, ves_ref, pts_ref, seg_ref, rad_ref, src_ref, *refs = refs
        *ins, k_ref, t_ref, rates_ref, par_ref, base_out, out_ref, pb, rr, sb = refs
        prepare(total_pts, total_segs, *ins, src_ref, rates_ref, par_ref, base_out, out_ref)
    else:
        pts_ref, seg_ref, rad_ref, src_ref, before_ref, k_ref, t_ref, pb, rr, sb = refs
    rows, cols = k_ref.shape
    solutes = src_ref.shape[0]
    rb = min(BUILD_ROWS, rows)
    pc = min(512, cols)
    rg = 16
    rr[...] = rad_ref[...] * rad_ref[...]
    sb[...] = src_ref[...].astype(BF16)

    def load_points(r):
        p = pts_ref[:, pl.ds(pl.multiple_of(part * rows + r * rb, rb), rb)]
        p = jnp.concatenate([p, jnp.zeros((5, rb), F32)], axis=0)
        pt = jnp.transpose(p)
        for q in range(3):
            pb[q] = jnp.broadcast_to(pt[:, q : q + 1], (rb, LANES))

    def make(r, c):
        for g in range(rb // rg):
            where = pl.ds(pl.multiple_of(r * rb + g * rg, rg), rg)
            px, py, pz = (pb[q, g * rg : (g + 1) * rg, :] for q in range(3))
            for t in range(0, pc // LANES, 2):
                first = c * pc + t * LANES
                pair = []
                for u in (0, 1):
                    at_cols = slice(first + u * LANES, first + (u + 1) * LANES)
                    dx = px - seg_ref[0:1, at_cols]
                    dy = py - seg_ref[1:2, at_cols]
                    dz = pz - seg_ref[2:3, at_cols]
                    pair.append(lax.rsqrt(((dx * dx + dy * dy) + dz * dz) + rr[:, at_cols]))
                k_ref[where, first : first + 2 * LANES] = jnp.concatenate(pair, axis=1).astype(BF16)

    def multiply(r, c):
        piece = slice(c * pc, (c + 1) * pc)
        return lax.dot_general(
            sb[:, piece], k_ref[at(r, rb), piece], (((1,), (1,)), ((), ())),
            preferred_element_type=F32,
        )

    n_pc = cols // pc
    load_points(0)
    for c in range(n_pc):
        make(0, c)

    def body(r, carry):
        load_points(r)
        acc = None
        for c in range(n_pc):
            got = multiply(r - 1, c)
            acc = got if acc is None else acc + got
            make(r, c)
        t_ref[:, at(r - 1, rb)] = acc
        return carry

    lax.fori_loop(1, rows // rb, body, 0)
    acc = None
    for c in range(n_pc):
        got = multiply(rows // rb - 1, c)
        acc = got if acc is None else acc + got
    t_ref[:, rows - rb : rows] = acc
    if part == 0:
        t_ref[:, rows : rows + LANES] = lane_sum(src_ref, solutes, cols)


def tissue_kernel(part, n_k, *refs):
    k_refs, refs = refs[:n_k], refs[n_k:]
    if part == 0:
        core_ref, mine_ref, theirs_ref, cont_ref, flow_ref, t_ref, src_ref, out_ref, sb = refs
        join_kernel(core_ref, mine_ref, theirs_ref, src_ref)
        out_ref[...] = cont_ref[...] - src_ref[...] * flow_ref[...]
    else:
        src_ref, t_ref, sb = refs
    rows, cols = k_refs[0].shape
    solutes = src_ref.shape[0]
    sb[...] = src_ref[...].astype(BF16)
    rb = min(1024, rows)
    pc = min(1024, cols)
    for i, k_ref in enumerate(k_refs):
        for r in range(rows // rb):
            acc = None
            for c in range(cols // pc):
                piece = slice(c * pc, (c + 1) * pc)
                got = lax.dot_general(
                    sb[:, piece], k_ref[r * rb : (r + 1) * rb, piece], (((1,), (1,)), ((), ())),
                    preferred_element_type=F32,
                )
                acc = got if acc is None else acc + got
            t_ref[:, i * rows + r * rb : i * rows + (r + 1) * rb] = acc
    if part == 0:
        whole = len(k_refs) * rows
        t_ref[:, whole : whole + LANES] = lane_sum(src_ref, solutes, cols)


def join_kernel(core_ref, mine_ref, theirs_ref, src_ref):
    half = mine_ref.shape[1]
    core = core_ref[0]
    src_ref[:, at(core, half)] = mine_ref[...]
    src_ref[:, at(1 - core, half)] = theirs_ref[...]


def wall_kernel(part, last, n_k, n_t, *refs):
    k_refs, refs = refs[:n_k], refs[n_k:]
    own_refs, refs = refs[:n_t], refs[n_t:]
    got_refs, refs = refs[:n_t], refs[n_t:]
    rates_ref, par_ref, base_ref, *refs = refs
    if part == 0:
        wall_ref, level_ref, tmp = refs
    else:
        core_ref, before_ref, level_in, up_ref, keep_ref, send_ref, *more, tmp, wall_ref = refs
        level_ref = more[0] if last else None
    rows, cols = k_refs[0].shape
    whole = n_k * rows
    solutes = rates_ref.shape[0]
    hs, dn, base = par_ref[0], par_ref[1], base_ref[...]
    total = jnp.zeros((solutes, LANES), F32)
    for p in range(whole // LANES):
        here = slice(p * LANES, (p + 1) * LANES)
        which, first = divmod(p * LANES, whole // n_t)
        there = slice(first, first + LANES)
        level = base + (own_refs[which][:, there] + got_refs[which][:, there]) / dn
        rate = rates_ref[:, part * whole + p * LANES : part * whole + (p + 1) * LANES]
        sink = rate * level / (jnp.abs(level) + hs)
        total = total + sink
        tmp[:, here] = sink.astype(BF16)
        if part == 0:
            level_ref[:, here] = level
        elif last:
            level_ref[:, whole + p * LANES : whole + (p + 1) * LANES] = level
    if part != 0 and last:
        level_ref[:, 0:whole] = level_in[...]
    total = jnp.broadcast_to(jnp.sum(total, axis=1, keepdims=True), (solutes, LANES))
    rb = min(256, rows)

    if part == 0:
        wall_ref[:, 0:cols] = jnp.zeros((solutes, cols), F32)
        wall_ref[:, cols : cols + LANES] = total
    else:
        wall_ref[:, 0:cols] = before_ref[:, 0:cols]
        total = total + before_ref[:, cols : cols + LANES]
    for i, k_ref in enumerate(k_refs):

        def body(r, carry):
            wall_ref[:, 0:cols] += jnp.dot(
                tmp[:, pl.ds(pl.multiple_of(i * rows + r * rb, rb), rb)], k_ref[at(r, rb), :],
                preferred_element_type=F32,
            )
            return carry

        lax.fori_loop(0, rows // rb, body, 0)
    if part != 0:
        half = cols // 2
        core = core_ref[0]
        keep_ref[:, 0:half] = wall_ref[:, at(core, half)]
        send_ref[:, 0:half] = wall_ref[:, at(1 - core, half)]
        keep_ref[:, half : half + LANES] = total
        send_ref[:, half : half + LANES] = total


def gather_kernel(ves_ref, parent_ref, up_ref, out_ref, inflow_ref, cont_ref, joined):
    solutes, cols = out_ref.shape
    joined[:, 0:cols] = up_ref[...]
    joined[:, cols : 2 * cols] = out_ref[...]
    first = ves_ref[0] * cols
    tiles = cols // LANES

    def body(j, carry):
        here = at(j, LANES)
        parent = jnp.broadcast_to(parent_ref[0:1, here], (solutes, LANES))
        seg = first + j * LANES + lax.broadcasted_iota(jnp.int32, (solutes, LANES), 1)
        place = parent - (first - cols)
        lane = lax.bitwise_and(place, LANES - 1)
        tile = lax.shift_right_arithmetic(place, 7) - j
        acc = inflow_ref[:, here]
        tile = jnp.where(parent == seg, -1, tile)
        for t in range(tiles + 1):
            got = jnp.take_along_axis(joined[:, at(j + t, LANES)], lane, axis=1)
            acc = jnp.where(tile == t, got, acc)
        cont_ref[:, here] = acc
        return carry

    lax.fori_loop(0, tiles, body, 0)


def update_kernel(
    total_pts, total_segs, core_ref, a_ref, b_ref, own_ref, got_ref, src_ref, cont_ref, cond_ref,
    par_ref, base_ref, new_ref, base_out
):
    half = new_ref.shape[1]
    rows = own_ref.shape[1] - LANES
    core = core_ref[0]
    dp = par_ref[2]
    for p in range(half // LANES):
        here = slice(p * LANES, (p + 1) * LANES)
        there = at(core * (half // LANES) + p, LANES)
        wall = (a_ref[:, here] + b_ref[:, here]) / dp
        new_ref[:, here] = RELAX * src_ref[:, there] + RELAX * cond_ref[:, there] * (
            cont_ref[:, there] - wall
        )
    sink_total = a_ref[:, half : half + LANES] + b_ref[:, half : half + LANES]
    source_total = own_ref[:, rows : rows + LANES] + got_ref[:, rows : rows + LANES]
    base_out[...] = base_ref[...] + BALANCE * (
        source_total / total_segs - sink_total / total_pts
    )


def body(
    point_xyz,
    point_cell,
    seg_xyz,
    seg_radius,
    conductance,
    flow_inv,
    parent,
    inflow,
    rate_table,
    half_sat,
    diffusivity,
    base_level,
    sources,
    contents,
):
    pts = point_xyz.shape[1]
    cols = seg_xyz.shape[1]
    solutes = sources.shape[0]
    n_tis = lax.axis_size("tis")
    n_ves = lax.axis_size("ves")
    total_pts = pts * n_tis
    total_segs = cols * n_ves
    rows = pts // PARTS
    half = cols // 2
    tis = lax.axis_index("tis")
    core = (tis % 2).astype(jnp.int32).reshape(1)
    ves = lax.axis_index("ves").astype(jnp.int32).reshape(1)

    def swap(value, bit):
        return lax.ppermute(value, "tis", [(i, i ^ bit) for i in range(n_tis)])

    def from_behind(value):
        return lax.ppermute(value, "ves", [(i, i + 1) for i in range(n_ves - 1)])

    def across(value):
        if n_ves == 2:
            return value, lax.ppermute(value, "ves", [(0, 1), (1, 0)])
        return lax.psum(value, "ves"), jnp.zeros_like(value)

    cond = conductance.reshape(1, cols)
    flow = flow_inv.reshape(1, cols)
    par_row = parent.reshape(1, cols)

    chunk = rows // CHUNKS
    pieces = [[None] * CHUNKS for _ in range(PARTS)]
    level = None
    for sweep in range(ITERS):
        last = sweep == ITERS - 1
        own, got = [[] for _ in range(PARTS)], [[] for _ in range(PARTS)]
        for part in range(PARTS):
            if sweep == 0:
                for i in range(CHUNKS):
                    index = part * CHUNKS + i
                    ins = [
                        ("h", point_xyz), ("h", seg_xyz), ("h", seg_radius.reshape(1, cols)),
                        ("h", sources),
                    ]
                    outs = [
                        pltpu.VMEM((chunk, cols), BF16),
                        shape(solutes, chunk + (LANES if index == 0 else 0)),
                    ]
                    if index == 0:
                        ins = [("s", core), ("s", ves)] + ins + [
                            ("h", rate_table), ("h", point_cell.reshape(1, pts)), ("hs", half_sat),
                            ("hs", diffusivity), ("hs", base_level), ("h", contents), ("h", flow),
                        ]
                        outs += [
                            shape(solutes, pts), shape(3, solutes, LANES), shape(solutes, LANES),
                            shape(solutes, cols),
                        ]
                    else:
                        ins += [("v", t)]
                    pieces[part][i], t, *more = call(
                        functools.partial(
                            build_kernel, index, float(total_pts), float(total_segs)
                        ),
                        outs,
                        ins,
                        f"build{index}",
                        scratch=[
                            pltpu.VMEM((3, min(BUILD_ROWS, chunk), LANES), F32),
                            pltpu.VMEM((1, cols), F32), pltpu.VMEM((solutes, cols), BF16),
                        ],
                        limit=BUILD_LIMIT,
                        flops=10 * chunk * cols,
                        bytes_accessed=20_000_000,
                    )
                    if index == 0:
                        rates, par, base, outflow = more
                        upstream = from_behind(outflow)
                    mine, other = across(t)
                    own[part].append(mine)
                    got[part].append(other)
            else:
                outs = [shape(solutes, rows + (LANES if part == 0 else 0))]
                ins = [("k", piece) for piece in pieces[part]]
                if part == 0:
                    outs += [shape(solutes, cols)] * 2
                    ins += [
                        ("s", core), ("v", new), ("v", theirs), ("v", contents), ("v", flow)
                    ]
                else:
                    ins += [("v", sources)]
                t, *more = call(
                    functools.partial(tissue_kernel, part, CHUNKS),
                    outs,
                    ins,
                    f"tissue{part}",
                    limit=18,
                    scratch=[pltpu.VMEM((solutes, cols), BF16)],
                    flops=2 * solutes * rows * cols,
                    bytes_accessed=10_000_000,
                )
                if part == 0:
                    sources, outflow = more
                    upstream = from_behind(outflow)
                mine, other = across(t)
                own[part].append(mine)
                got[part].append(other)

        def wall_ins(part):
            return (
                [("k", piece) for piece in pieces[part]]
                + [("v", t) for t in own[part]]
                + [("v", t) for t in got[part]]
                + [("v", rates), ("v", par), ("v", base)]
            )

        wall, level = call(
            functools.partial(wall_kernel, 0, last, CHUNKS, len(own[0])),
            [shape(solutes, cols + LANES), shape(solutes, rows)],
            wall_ins(0),
            "wall0",
            limit=18,
            scratch=[pltpu.VMEM((solutes, rows), BF16)],
            flops=2 * solutes * rows * cols,
            bytes_accessed=10_000_000,
        )
        keep, send, *more = call(
            functools.partial(wall_kernel, 1, last, CHUNKS, len(own[1])),
            [shape(solutes, half + LANES)] * 2 + ([shape(solutes, pts)] if last else []),
            wall_ins(1) + [("s", core), ("v", wall), ("v", level), ("v", upstream)],
            "wall1",
            limit=18,
            scratch=[pltpu.VMEM((solutes, rows), BF16), pltpu.VMEM((solutes, cols), F32)],
            flops=2 * solutes * rows * cols,
            bytes_accessed=10_000_000,
        )
        if last:
            level = more[0]
        (new_contents,) = call(
            gather_kernel,
            [shape(solutes, cols)],
            [("s", ves), ("v", par_row), ("v", upstream), ("v", outflow), ("v", inflow)],
            "gather",
            scratch=[pltpu.VMEM((solutes, 2 * cols), F32)],
            flops=solutes * cols * 33,
            bytes_accessed=8_000_000,
        )
        theirs = swap(send, 1)
        bit = 2
        while bit < n_tis:
            keep = keep + theirs
            theirs = swap(keep, bit)
            bit *= 2
        new, base = call(
            functools.partial(update_kernel, float(total_pts), float(total_segs)),
            [shape(solutes, half), shape(solutes, LANES)],
            [
                ("s", core), ("v", keep), ("v", theirs), ("v", own[0][0]), ("v", got[0][0]),
                ("v", sources), ("v", new_contents), ("v", cond), ("v", par), ("v", base),
            ],
            "update",
        )
        contents = new_contents
        theirs = swap(new, 1)
    (sources,) = call(
        join_kernel,
        [shape(solutes, cols)],
        [("s", core), ("v", new), ("v", theirs)],
        "join",
    )
    return (level, sources, contents)


def solution(mesh):
    return jax.shard_map(
        body,
        mesh=mesh,
        in_specs=(
            P(None, "tis"),
            P("tis"),
            P(None, "ves"),
            P("ves"),
            P("ves"),
            P("ves"),
            P("ves"),
            P(None, "ves"),
            P(),
            P(),
            P(),
            P(),
            P(None, "ves"),
            P(None, "ves"),
        ),
        out_specs=(P(None, "tis"), P(None, "ves"), P(None, "ves")),
        check_vma=False,
    )
```

```python
import functools

import jax
import jax.numpy as jnp
from jax import lax
from jax.experimental import pallas as pl
from jax.experimental.pallas import tpu as pltpu
from jax.sharding import PartitionSpec as P

ITERS = 3

RELAX = 0.5
BALANCE = 0.5
LANES = 128
PARTS = 2
CHUNKS = 2
BUILD_ROWS = 128
BUILD_LIMIT = 21


VM = pl.BlockSpec(memory_space=pltpu.VMEM)
SM = pl.BlockSpec(memory_space=pltpu.SMEM)
F32 = jnp.float32
BF16 = jnp.bfloat16


def call(kernel, outs, ins, name, scratch=(), limit=4, flops=0, bytes_accessed=0):
    specs = [SM if space in ("s", "hs") else VM for space, _ in ins]
    pinned = {"k": pltpu.VMEM, "h": pltpu.HBM, "hs": pltpu.HBM}
    arrays = [
        pltpu.with_memory_space_constraint(value, pinned[space]) if space in pinned else value
        for space, value in ins
    ]
    return pl.pallas_call(
        kernel,
        out_shape=tuple(outs),
        in_specs=specs,
        out_specs=(VM,) * len(outs),
        scratch_shapes=list(scratch),
        compiler_params=pltpu.CompilerParams(vmem_limit_bytes=limit << 20),
        cost_estimate=pl.CostEstimate(
            flops=flops, bytes_accessed=bytes_accessed, transcendentals=0
        ),
        name=name,
    )(*arrays)


def shape(*dims):
    return jax.ShapeDtypeStruct(dims, F32)


def at(block, size):
    return pl.ds(pl.multiple_of(block * size, size), size)


def lane_sum(ref, solutes, cols):
    acc = ref[:, 0:LANES]
    for tile in range(1, cols // LANES):
        acc = acc + ref[:, tile * LANES : (tile + 1) * LANES]
    return jnp.broadcast_to(jnp.sum(acc, axis=1, keepdims=True), (solutes, LANES))


def prepare(
    total_pts, total_segs, table_ref, cell_ref, hs_ref, diff_ref, base_ref, cont_ref, flow_ref,
    src_ref, rates_ref, par_ref, base_out, out_ref
):
    solutes, pts = rates_ref.shape
    row = lax.broadcasted_iota(jnp.int32, (solutes, LANES), 0)

    def spread(ref):
        acc = jnp.full((solutes, LANES), ref[0], F32)
        for s in range(1, solutes):
            acc = jnp.where(row == s, ref[s], acc)
        return acc

    diff = spread(diff_ref)
    par_ref[0] = spread(hs_ref)
    par_ref[1] = diff * total_segs
    par_ref[2] = diff * total_pts
    base_out[...] = spread(base_ref)
    out_ref[...] = cont_ref[...] - src_ref[...] * flow_ref[...]
    n_cells = table_ref.shape[1]
    tiles = pl.cdiv(n_cells, LANES)
    spare = tiles * LANES - n_cells
    table = table_ref[...]
    if spare:
        table = jnp.concatenate([table, jnp.zeros((solutes, spare), F32)], axis=1)
    for p in range(pts // LANES):
        cols = slice(p * LANES, (p + 1) * LANES)
        cell = jnp.broadcast_to(cell_ref[0:1, cols], (solutes, LANES))
        lane = lax.bitwise_and(cell, LANES - 1)
        acc = jnp.take_along_axis(table[:, 0:LANES], lane, axis=1)
        for t in range(1, tiles):
            got = jnp.take_along_axis(table[:, t * LANES : (t + 1) * LANES], lane, axis=1)
            acc = jnp.where(lax.shift_right_logical(cell, 7) == t, got, acc)
        rates_ref[:, cols] = acc


def build_kernel(part, total_pts, total_segs, n_k, *refs):
    if part == 0:
        core_ref, ves_ref, pts_ref, seg_ref, rad_ref, src_ref, *refs = refs
        ins, refs = refs[:7], refs[7:]
        k_refs, refs = refs[:n_k], refs[n_k:]
        t_ref, rates_ref, par_ref, base_out, out_ref, pb, rr, sb = refs
        prepare(total_pts, total_segs, *ins, src_ref, rates_ref, par_ref, base_out, out_ref)
    else:
        pts_ref, seg_ref, rad_ref, src_ref, before_ref, *refs = refs
        k_refs, refs = refs[:n_k], refs[n_k:]
        t_ref, pb, rr, sb = refs
    rows, cols = k_refs[0].shape
    whole = n_k * rows
    solutes = src_ref.shape[0]
    rb = min(BUILD_ROWS, rows)
    pc = cols
    rg = 16
    n_pc = cols // pc
    n_rb = rows // rb
    rr[...] = rad_ref[...] * rad_ref[...]
    sb[...] = src_ref[...].astype(BF16)

    def load_points(block):
        p = pts_ref[:, pl.ds(pl.multiple_of(part * whole + block * rb, rb), rb)]
        p = jnp.concatenate([p, jnp.zeros((5, rb), F32)], axis=0)
        pt = jnp.transpose(p)
        for q in range(3):
            pb[q] = jnp.broadcast_to(pt[:, q : q + 1], (rb, LANES))

    def tiles(k_ref, where, points, first, count):
        px, py, pz = points
        for t in range(0, count, 2):
            pair = []
            for u in (0, 1):
                here = slice(first + (t + u) * LANES, first + (t + u + 1) * LANES)
                dx = px - seg_ref[0:1, here]
                dy = py - seg_ref[1:2, here]
                dz = pz - seg_ref[2:3, here]
                pair.append(lax.rsqrt(((dx * dx + dy * dy) + dz * dz) + rr[:, here]))
            both = slice(first + t * LANES, first + (t + 2) * LANES)
            k_ref[where, both] = jnp.concatenate(pair, axis=1).astype(BF16)

    def make(i, r, c):
        for g in range(rb // rg):
            where = pl.ds(pl.multiple_of(r * rb + g * rg, rg), rg)
            points = [pb[q, g * rg : (g + 1) * rg, :] for q in range(3)]
            tiles(k_refs[i], where, points, c * pc, pc // LANES)

    def multiply(i, r, c):
        piece = slice(c * pc, (c + 1) * pc)
        return lax.dot_general(
            sb[:, piece], k_refs[i][at(r, rb), piece], (((1,), (1,)), ((), ())),
            preferred_element_type=F32,
        )

    def step(done, made):
        acc = None
        for c in range(n_pc):
            got = multiply(*done, c)
            acc = got if acc is None else acc + got
            if made is not None:
                make(*made, c)
        t_ref[:, pl.ds(pl.multiple_of(done[0] * rows + done[1] * rb, rb), rb)] = acc

    load_points(0)

    def first(g, carry):
        where = at(g, rg)
        tiles(k_refs[0], where, [pb[q, where, :] for q in range(3)], 0, cols // LANES)
        return carry

    lax.fori_loop(0, rb // rg, first, 0)
    for i in range(n_k):
        if i:
            load_points(i * n_rb)
            step((i - 1, n_rb - 1), (i, 0))

        def body(r, carry):
            load_points(i * n_rb + r)
            step((i, r - 1), (i, r))
            return carry

        lax.fori_loop(1, n_rb, body, 0)
    step((n_k - 1, n_rb - 1), None)
    if part == 0:
        t_ref[:, whole : whole + LANES] = lane_sum(src_ref, solutes, cols)


def tissue_kernel(part, n_k, *refs):
    k_refs, refs = refs[:n_k], refs[n_k:]
    if part == 0:
        core_ref, mine_ref, theirs_ref, cont_ref, flow_ref, t_ref, src_ref, out_ref, sb = refs
        join_kernel(core_ref, mine_ref, theirs_ref, src_ref)
        out_ref[...] = cont_ref[...] - src_ref[...] * flow_ref[...]
    else:
        src_ref, t_ref, sb = refs
    rows, cols = k_refs[0].shape
    solutes = src_ref.shape[0]
    sb[...] = src_ref[...].astype(BF16)
    rb = min(1024, rows)
    pc = min(1024, cols)
    for i, k_ref in enumerate(k_refs):
        for r in range(rows // rb):
            acc = None
            for c in range(cols // pc):
                piece = slice(c * pc, (c + 1) * pc)
                got = lax.dot_general(
                    sb[:, piece], k_ref[r * rb : (r + 1) * rb, piece], (((1,), (1,)), ((), ())),
                    preferred_element_type=F32,
                )
                acc = got if acc is None else acc + got
            t_ref[:, i * rows + r * rb : i * rows + (r + 1) * rb] = acc
    if part == 0:
        whole = len(k_refs) * rows
        t_ref[:, whole : whole + LANES] = lane_sum(src_ref, solutes, cols)


def join_kernel(core_ref, mine_ref, theirs_ref, src_ref):
    half = mine_ref.shape[1]
    core = core_ref[0]
    src_ref[:, at(core, half)] = mine_ref[...]
    src_ref[:, at(1 - core, half)] = theirs_ref[...]


def sinks(part, own_refs, got_refs, rates_ref, par_ref, base_ref, tmp, level_ref, first):
    whole = tmp.shape[1]
    solutes = rates_ref.shape[0]
    hs, dn, base = par_ref[0], par_ref[1], base_ref[...]
    total = jnp.zeros((solutes, LANES), F32)
    for p in range(0, whole, LANES):
        here = slice(p, p + LANES)
        level = base + (own_refs[:, here] + got_refs[:, here]) / dn
        rate = rates_ref[:, part * whole + p : part * whole + p + LANES]
        sink = rate * level / (jnp.abs(level) + hs)
        total = total + sink
        tmp[:, here] = sink.astype(BF16)
        if level_ref is not None:
            level_ref[:, first + p : first + p + LANES] = level
    return jnp.broadcast_to(jnp.sum(total, axis=1, keepdims=True), (solutes, LANES))


def add_wall(acc_ref, tmp, k_refs, first):
    width = acc_ref.shape[1] - LANES
    rows = k_refs[0].shape[0]
    rb = min(256, rows)
    for i, k_ref in enumerate(k_refs):

        def body(r, carry):
            acc_ref[:, 0:width] += jnp.dot(
                tmp[:, pl.ds(pl.multiple_of(i * rows + r * rb, rb), rb)],
                k_ref[at(r, rb), pl.ds(first, width)],
                preferred_element_type=F32,
            )
            return carry

        lax.fori_loop(0, rows // rb, body, 0)


def wall_kernel(n_k, *refs):
    k_refs, refs = refs[:n_k], refs[n_k:]
    own_ref, got_ref, rates_ref, par_ref, base_ref, wall_ref, level_ref, tmp = refs
    solutes, cols = rates_ref.shape[0], k_refs[0].shape[1]
    total = sinks(0, own_ref, got_ref, rates_ref, par_ref, base_ref, tmp, level_ref, 0)
    wall_ref[:, 0:cols] = jnp.zeros((solutes, cols), F32)
    wall_ref[:, cols : cols + LANES] = total
    add_wall(wall_ref, tmp, k_refs, 0)


def send_kernel(last, n_k, *refs):
    k_refs, refs = refs[:n_k], refs[n_k:]
    (
        own_ref, got_ref, rates_ref, par_ref, base_ref, core_ref, before_ref, level_in, up_ref,
        send_ref, tmp, *more,
    ) = refs
    cols = k_refs[0].shape[1]
    whole = tmp.shape[1]
    half = cols // 2
    level_ref = more[0] if last else None
    total = sinks(1, own_ref, got_ref, rates_ref, par_ref, base_ref, tmp, level_ref, whole)
    if last:
        level_ref[:, 0:whole] = level_in[...]
    other = 1 - core_ref[0]
    send_ref[:, 0:half] = before_ref[:, at(other, half)]
    send_ref[:, half : half + LANES] = before_ref[:, cols : cols + LANES] + total
    add_wall(send_ref, tmp, k_refs, pl.multiple_of(other * half, half))


def keep_kernel(n_k, *refs):
    k_refs, refs = refs[:n_k], refs[n_k:]
    core_ref, before_ref, send_ref, tmp, keep_ref = refs
    half = k_refs[0].shape[1] // 2
    core = core_ref[0]
    keep_ref[:, 0:half] = before_ref[:, at(core, half)]
    keep_ref[:, half : half + LANES] = send_ref[:, half : half + LANES]
    add_wall(keep_ref, tmp, k_refs, pl.multiple_of(core * half, half))


def gather_kernel(ves_ref, parent_ref, up_ref, out_ref, inflow_ref, *refs):
    *cont_refs, joined = refs
    solutes, cols = out_ref.shape
    joined[:, 0:cols] = up_ref[...]
    joined[:, cols : 2 * cols] = out_ref[...]
    first = ves_ref[0] * cols
    tiles = cols // LANES

    def body(j, carry):
        here = at(j, LANES)
        parent = jnp.broadcast_to(parent_ref[0:1, here], (solutes, LANES))
        seg = first + j * LANES + lax.broadcasted_iota(jnp.int32, (solutes, LANES), 1)
        place = parent - (first - cols)
        lane = lax.bitwise_and(place, LANES - 1)
        tile = lax.shift_right_arithmetic(place, 7) - j
        acc = inflow_ref[:, here]
        tile = jnp.where(parent == seg, -1, tile)
        for t in range(tiles + 1):
            got = jnp.take_along_axis(joined[:, at(j + t, LANES)], lane, axis=1)
            acc = jnp.where(tile == t, got, acc)
        for cont_ref in cont_refs:
            cont_ref[:, here] = acc
        return carry

    lax.fori_loop(0, tiles, body, 0)


def update_kernel(
    total_pts, total_segs, core_ref, a_ref, b_ref, own_ref, got_ref, src_ref, cont_ref, cond_ref,
    par_ref, base_ref, new_ref, *base_out
):
    half = new_ref.shape[1]
    rows = own_ref.shape[1] - LANES
    core = core_ref[0]
    dp = par_ref[2]
    for p in range(half // LANES):
        here = slice(p * LANES, (p + 1) * LANES)
        there = at(core * (half // LANES) + p, LANES)
        wall = (a_ref[:, here] + b_ref[:, here]) / dp
        new_ref[:, here] = RELAX * src_ref[:, there] + RELAX * cond_ref[:, there] * (
            cont_ref[:, there] - wall
        )
    if base_out:
        sink_total = a_ref[:, half : half + LANES] + b_ref[:, half : half + LANES]
        source_total = own_ref[:, rows : rows + LANES] + got_ref[:, rows : rows + LANES]
        base_out[0][...] = base_ref[...] + BALANCE * (
            source_total / total_segs - sink_total / total_pts
        )


def body(
    point_xyz,
    point_cell,
    seg_xyz,
    seg_radius,
    conductance,
    flow_inv,
    parent,
    inflow,
    rate_table,
    half_sat,
    diffusivity,
    base_level,
    sources,
    contents,
):
    pts = point_xyz.shape[1]
    cols = seg_xyz.shape[1]
    solutes = sources.shape[0]
    n_tis = lax.axis_size("tis")
    n_ves = lax.axis_size("ves")
    total_pts = pts * n_tis
    total_segs = cols * n_ves
    rows = pts // PARTS
    half = cols // 2
    tis = lax.axis_index("tis")
    core = (tis % 2).astype(jnp.int32).reshape(1)
    ves = lax.axis_index("ves").astype(jnp.int32).reshape(1)

    def swap(value, bit):
        return lax.ppermute(value, "tis", [(i, i ^ bit) for i in range(n_tis)])

    def from_behind(value):
        return lax.ppermute(value, "ves", [(i, i + 1) for i in range(n_ves - 1)])

    def across(value):
        if n_ves == 2:
            return value, lax.ppermute(value, "ves", [(0, 1), (1, 0)])
        return lax.psum(value, "ves"), jnp.zeros_like(value)

    cond = conductance.reshape(1, cols)
    flow = flow_inv.reshape(1, cols)
    par_row = parent.reshape(1, cols)

    chunk = rows // CHUNKS
    pieces = [[None] * CHUNKS for _ in range(PARTS)]
    level = None
    for sweep in range(ITERS):
        last = sweep == ITERS - 1
        own, got = [], []
        for part in range(PARTS):
            if sweep == 0:
                ins = [
                    ("h", point_xyz), ("h", seg_xyz), ("h", seg_radius.reshape(1, cols)),
                    ("h", sources),
                ]
                outs = [pltpu.VMEM((chunk, cols), BF16)] * CHUNKS + [
                    shape(solutes, rows + (LANES if part == 0 else 0))
                ]
                if part == 0:
                    ins = [("s", core), ("s", ves)] + ins + [
                        ("h", rate_table), ("h", point_cell.reshape(1, pts)), ("hs", half_sat),
                        ("hs", diffusivity), ("hs", base_level), ("h", contents), ("h", flow),
                    ]
                    outs += [
                        shape(solutes, pts), shape(3, solutes, LANES), shape(solutes, LANES),
                        shape(solutes, cols),
                    ]
                else:
                    ins += [("v", t)]
                *made, = call(
                    functools.partial(
                        build_kernel, part, float(total_pts), float(total_segs), CHUNKS
                    ),
                    outs,
                    ins,
                    f"build{part}",
                    scratch=[
                        pltpu.VMEM((3, min(BUILD_ROWS, chunk), LANES), F32),
                        pltpu.VMEM((1, cols), F32), pltpu.VMEM((solutes, cols), BF16),
                    ],
                    limit=BUILD_LIMIT,
                    flops=10 * rows * cols,
                    bytes_accessed=40_000_000,
                )
                pieces[part], t, more = made[:CHUNKS], made[CHUNKS], made[CHUNKS + 1 :]
                if part == 0:
                    rates, par, base, outflow = more
                    upstream = from_behind(outflow)
            else:
                outs = [shape(solutes, rows + (LANES if part == 0 else 0))]
                ins = [("k", piece) for piece in pieces[part]]
                if part == 0:
                    outs += [shape(solutes, cols)] * 2
                    ins += [
                        ("s", core), ("v", new), ("v", theirs), ("v", contents), ("v", flow)
                    ]
                else:
                    ins += [("v", sources)]
                t, *more = call(
                    functools.partial(tissue_kernel, part, CHUNKS),
                    outs,
                    ins,
                    f"tissue{part}",
                    limit=18,
                    scratch=[pltpu.VMEM((solutes, cols), BF16)],
                    flops=2 * solutes * rows * cols,
                    bytes_accessed=10_000_000,
                )
                if part == 0:
                    sources, outflow = more
                    upstream = from_behind(outflow)
            mine, other = across(t)
            own.append(mine)
            got.append(other)

        def wall_ins(part):
            return [("k", piece) for piece in pieces[part]] + [
                ("v", own[part]), ("v", got[part]), ("v", rates), ("v", par), ("v", base),
            ]

        wall, level = call(
            functools.partial(wall_kernel, CHUNKS),
            [shape(solutes, cols + LANES), shape(solutes, rows)],
            wall_ins(0),
            "wall0",
            limit=18,
            scratch=[pltpu.VMEM((solutes, rows), BF16)],
            flops=2 * solutes * rows * cols,
            bytes_accessed=10_000_000,
        )
        send, sink, *more = call(
            functools.partial(send_kernel, last, CHUNKS),
            [shape(solutes, half + LANES), jax.ShapeDtypeStruct((solutes, rows), BF16)]
            + ([shape(solutes, pts)] if last else []),
            wall_ins(1) + [("s", core), ("v", wall), ("v", level), ("v", upstream)],
            "send",
            limit=18,
            flops=solutes * rows * cols,
            bytes_accessed=5_000_000,
        )
        theirs = swap(send, 1)
        (keep,) = call(
            functools.partial(keep_kernel, CHUNKS),
            [shape(solutes, half + LANES)],
            [("k", piece) for piece in pieces[1]]
            + [("s", core), ("v", wall), ("v", send), ("v", sink)],
            "keep",
            limit=18,
            flops=solutes * rows * cols,
            bytes_accessed=5_000_000,
        )
        if last:
            level = more[0]
        new_contents, *copy = call(
            gather_kernel,
            [shape(solutes, cols)] * (2 if last else 1),
            [("s", ves), ("v", par_row), ("v", upstream), ("v", outflow), ("v", inflow)],
            "gather",
            scratch=[pltpu.VMEM((solutes, 2 * cols), F32)],
            flops=solutes * cols * 33,
            bytes_accessed=8_000_000,
        )
        bit = 2
        while bit < n_tis:
            keep = keep + theirs
            theirs = swap(keep, bit)
            bit *= 2
        new, *rest = call(
            functools.partial(update_kernel, float(total_pts), float(total_segs)),
            [shape(solutes, half)] + ([] if last else [shape(solutes, LANES)]),
            [
                ("s", core), ("v", keep), ("v", theirs), ("v", own[0]), ("v", got[0]),
                ("v", sources), ("v", new_contents), ("v", cond), ("v", par), ("v", base),
            ],
            "update",
        )
        base = base if last else rest[0]
        contents = copy[0] if last else new_contents
        theirs = swap(new, 1)
    (sources,) = call(
        join_kernel,
        [shape(solutes, cols)],
        [("s", core), ("v", new), ("v", theirs)],
        "join",
    )
    return (level, sources, contents)


def solution(mesh):
    return jax.shard_map(
        body,
        mesh=mesh,
        in_specs=(
            P(None, "tis"),
            P("tis"),
            P(None, "ves"),
            P("ves"),
            P("ves"),
            P("ves"),
            P("ves"),
            P(None, "ves"),
            P(),
            P(),
            P(),
            P(),
            P(None, "ves"),
            P(None, "ves"),
        ),
        out_specs=(P(None, "tis"), P(None, "ves"), P(None, "ves")),
        check_vma=False,
    )
```

```python
import functools

import jax
import jax.numpy as jnp
from jax import lax
from jax.experimental import pallas as pl
from jax.experimental.pallas import tpu as pltpu
from jax.sharding import PartitionSpec as P

ITERS = 3

RELAX = 0.5
BALANCE = 0.5
LANES = 128
PARTS = 2
CHUNKS = 2
BUILD_ROWS = 128
BUILD_LIMIT = 21


VM = pl.BlockSpec(memory_space=pltpu.VMEM)
SM = pl.BlockSpec(memory_space=pltpu.SMEM)
F32 = jnp.float32
BF16 = jnp.bfloat16


def call(kernel, outs, ins, name, scratch=(), limit=4, flops=0, bytes_accessed=0):
    specs = [SM if space in ("s", "hs") else VM for space, _ in ins]
    pinned = {"k": pltpu.VMEM, "h": pltpu.HBM, "hs": pltpu.HBM}
    arrays = [
        pltpu.with_memory_space_constraint(value, pinned[space]) if space in pinned else value
        for space, value in ins
    ]
    return pl.pallas_call(
        kernel,
        out_shape=tuple(outs),
        in_specs=specs,
        out_specs=(VM,) * len(outs),
        scratch_shapes=list(scratch),
        compiler_params=pltpu.CompilerParams(vmem_limit_bytes=limit << 20),
        cost_estimate=pl.CostEstimate(
            flops=flops, bytes_accessed=bytes_accessed, transcendentals=0
        ),
        name=name,
    )(*arrays)


def shape(*dims):
    return jax.ShapeDtypeStruct(dims, F32)


def at(block, size):
    return pl.ds(pl.multiple_of(block * size, size), size)


def lane_sum(ref, solutes, cols):
    acc = ref[:, 0:LANES]
    for tile in range(1, cols // LANES):
        acc = acc + ref[:, tile * LANES : (tile + 1) * LANES]
    return jnp.broadcast_to(jnp.sum(acc, axis=1, keepdims=True), (solutes, LANES))


def prepare(
    total_pts, total_segs, table_ref, cell_ref, hs_ref, diff_ref, base_ref, cont_ref, flow_ref,
    src_ref, rates_ref, par_ref, base_out, out_ref
):
    solutes, pts = rates_ref.shape
    row = lax.broadcasted_iota(jnp.int32, (solutes, LANES), 0)

    def spread(ref):
        acc = jnp.full((solutes, LANES), ref[0], F32)
        for s in range(1, solutes):
            acc = jnp.where(row == s, ref[s], acc)
        return acc

    diff = spread(diff_ref)
    par_ref[0] = spread(hs_ref)
    par_ref[1] = diff * total_segs
    par_ref[2] = diff * total_pts
    base_out[...] = spread(base_ref)
    out_ref[...] = cont_ref[...] - src_ref[...] * flow_ref[...]
    n_cells = table_ref.shape[1]
    tiles = pl.cdiv(n_cells, LANES)
    spare = tiles * LANES - n_cells
    table = table_ref[...]
    if spare:
        table = jnp.concatenate([table, jnp.zeros((solutes, spare), F32)], axis=1)
    for p in range(pts // LANES):
        cols = slice(p * LANES, (p + 1) * LANES)
        cell = jnp.broadcast_to(cell_ref[0:1, cols], (solutes, LANES))
        lane = lax.bitwise_and(cell, LANES - 1)
        acc = jnp.take_along_axis(table[:, 0:LANES], lane, axis=1)
        for t in range(1, tiles):
            got = jnp.take_along_axis(table[:, t * LANES : (t + 1) * LANES], lane, axis=1)
            acc = jnp.where(lax.shift_right_logical(cell, 7) == t, got, acc)
        rates_ref[:, cols] = acc


def build_kernel(part, total_pts, total_segs, n_k, *refs):
    if part == 0:
        core_ref, ves_ref, pts_ref, seg_ref, rad_ref, src_ref, *refs = refs
        ins, refs = refs[:7], refs[7:]
        k_refs, refs = refs[:n_k], refs[n_k:]
        t_ref, rates_ref, par_ref, base_out, out_ref, pb, rr, sb = refs
        prepare(total_pts, total_segs, *ins, src_ref, rates_ref, par_ref, base_out, out_ref)
    else:
        pts_ref, seg_ref, rad_ref, src_ref, before_ref, *refs = refs
        k_refs, refs = refs[:n_k], refs[n_k:]
        t_ref, pb, rr, sb = refs
    rows, cols = k_refs[0].shape
    whole = n_k * rows
    solutes = src_ref.shape[0]
    rb = min(BUILD_ROWS, rows)
    pc = cols
    rg = 16
    n_pc = cols // pc
    n_rb = rows // rb
    rr[...] = rad_ref[...] * rad_ref[...]
    sb[...] = src_ref[...].astype(BF16)

    def load_points(block):
        p = pts_ref[:, pl.ds(pl.multiple_of(part * whole + block * rb, rb), rb)]
        p = jnp.concatenate([p, jnp.zeros((5, rb), F32)], axis=0)
        pt = jnp.transpose(p)
        for q in range(3):
            pb[q] = jnp.broadcast_to(pt[:, q : q + 1], (rb, LANES))

    def tiles(k_ref, where, points, first, count):
        px, py, pz = points
        for t in range(0, count, 2):
            pair = []
            for u in (0, 1):
                here = slice(first + (t + u) * LANES, first + (t + u + 1) * LANES)
                dx = px - seg_ref[0:1, here]
                dy = py - seg_ref[1:2, here]
                dz = pz - seg_ref[2:3, here]
                pair.append(lax.rsqrt(((dx * dx + dy * dy) + dz * dz) + rr[:, here]))
            both = slice(first + t * LANES, first + (t + 2) * LANES)
            k_ref[where, both] = jnp.concatenate(pair, axis=1).astype(BF16)

    def make(i, r, c):
        for g in range(rb // rg):
            where = pl.ds(pl.multiple_of(r * rb + g * rg, rg), rg)
            points = [pb[q, g * rg : (g + 1) * rg, :] for q in range(3)]
            tiles(k_refs[i], where, points, c * pc, pc // LANES)

    def multiply(i, r, c):
        piece = slice(c * pc, (c + 1) * pc)
        return lax.dot_general(
            sb[:, piece], k_refs[i][at(r, rb), piece], (((1,), (1,)), ((), ())),
            preferred_element_type=F32,
        )

    def step(done, made):
        acc = None
        for c in range(n_pc):
            got = multiply(*done, c)
            acc = got if acc is None else acc + got
            if made is not None:
                make(*made, c)
        t_ref[:, pl.ds(pl.multiple_of(done[0] * rows + done[1] * rb, rb), rb)] = acc

    load_points(0)

    def first(g, carry):
        where = at(g, rg)
        tiles(k_refs[0], where, [pb[q, where, :] for q in range(3)], 0, cols // LANES)
        return carry

    lax.fori_loop(0, rb // rg, first, 0)
    for i in range(n_k):
        if i:
            load_points(i * n_rb)
            step((i - 1, n_rb - 1), (i, 0))

        def body(r, carry):
            load_points(i * n_rb + r)
            step((i, r - 1), (i, r))
            return carry

        lax.fori_loop(1, n_rb, body, 0)
    step((n_k - 1, n_rb - 1), None)
    if part == 0:
        t_ref[:, whole : whole + LANES] = lane_sum(src_ref, solutes, cols)


def tissue_kernel(part, n_k, *refs):
    k_refs, refs = refs[:n_k], refs[n_k:]
    if part == 0:
        core_ref, mine_ref, theirs_ref, cont_ref, flow_ref, t_ref, src_ref, out_ref, sb = refs
        join_kernel(core_ref, mine_ref, theirs_ref, src_ref)
        out_ref[...] = cont_ref[...] - src_ref[...] * flow_ref[...]
    else:
        src_ref, t_ref, sb = refs
    rows, cols = k_refs[0].shape
    solutes = src_ref.shape[0]
    sb[...] = src_ref[...].astype(BF16)
    rb = min(1024, rows)
    pc = min(1024, cols)
    for i, k_ref in enumerate(k_refs):
        for r in range(rows // rb):
            acc = None
            for c in range(cols // pc):
                piece = slice(c * pc, (c + 1) * pc)
                got = lax.dot_general(
                    sb[:, piece], k_ref[r * rb : (r + 1) * rb, piece], (((1,), (1,)), ((), ())),
                    preferred_element_type=F32,
                )
                acc = got if acc is None else acc + got
            t_ref[:, i * rows + r * rb : i * rows + (r + 1) * rb] = acc
    if part == 0:
        whole = len(k_refs) * rows
        t_ref[:, whole : whole + LANES] = lane_sum(src_ref, solutes, cols)


def join_kernel(core_ref, mine_ref, theirs_ref, src_ref):
    half = mine_ref.shape[1]
    core = core_ref[0]
    src_ref[:, at(core, half)] = mine_ref[...]
    src_ref[:, at(1 - core, half)] = theirs_ref[...]


def sinks(part, own_refs, got_refs, rates_ref, par_ref, base_ref, tmp, level_ref, first):
    whole = tmp.shape[1]
    solutes = rates_ref.shape[0]
    hs, dn, base = par_ref[0], par_ref[1], base_ref[...]
    total = jnp.zeros((solutes, LANES), F32)
    for p in range(0, whole, LANES):
        here = slice(p, p + LANES)
        level = base + (own_refs[:, here] + got_refs[:, here]) / dn
        rate = rates_ref[:, part * whole + p : part * whole + p + LANES]
        sink = rate * level / (jnp.abs(level) + hs)
        total = total + sink
        tmp[:, here] = sink.astype(BF16)
        if level_ref is not None:
            level_ref[:, first + p : first + p + LANES] = level
    return jnp.broadcast_to(jnp.sum(total, axis=1, keepdims=True), (solutes, LANES))


def add_wall(acc_ref, tmp, k_refs, first):
    width = acc_ref.shape[1] - LANES
    rows = k_refs[0].shape[0]
    for i, k_ref in enumerate(k_refs):
        acc_ref[:, 0:width] += jnp.dot(
            tmp[:, i * rows : (i + 1) * rows], k_ref[:, pl.ds(first, width)],
            preferred_element_type=F32,
        )


def wall_kernel(n_k, *refs):
    k_refs, refs = refs[:n_k], refs[n_k:]
    own_ref, got_ref, rates_ref, par_ref, base_ref, wall_ref, level_ref, tmp = refs
    solutes, cols = rates_ref.shape[0], k_refs[0].shape[1]
    total = sinks(0, own_ref, got_ref, rates_ref, par_ref, base_ref, tmp, level_ref, 0)
    wall_ref[:, 0:cols] = jnp.zeros((solutes, cols), F32)
    wall_ref[:, cols : cols + LANES] = total
    add_wall(wall_ref, tmp, k_refs, 0)


def send_kernel(last, n_k, *refs):
    k_refs, refs = refs[:n_k], refs[n_k:]
    (
        own_ref, got_ref, rates_ref, par_ref, base_ref, core_ref, before_ref, level_in, up_ref,
        send_ref, tmp, *more,
    ) = refs
    cols = k_refs[0].shape[1]
    whole = tmp.shape[1]
    half = cols // 2
    level_ref = more[0] if last else None
    total = sinks(1, own_ref, got_ref, rates_ref, par_ref, base_ref, tmp, level_ref, whole)
    if last:
        level_ref[:, 0:whole] = level_in[...]
    other = 1 - core_ref[0]
    send_ref[:, 0:half] = before_ref[:, at(other, half)]
    send_ref[:, half : half + LANES] = before_ref[:, cols : cols + LANES] + total
    add_wall(send_ref, tmp, k_refs, pl.multiple_of(other * half, half))


def keep_kernel(n_k, *refs):
    k_refs, refs = refs[:n_k], refs[n_k:]
    core_ref, before_ref, send_ref, tmp, keep_ref = refs
    half = k_refs[0].shape[1] // 2
    core = core_ref[0]
    keep_ref[:, 0:half] = before_ref[:, at(core, half)]
    keep_ref[:, half : half + LANES] = send_ref[:, half : half + LANES]
    add_wall(keep_ref, tmp, k_refs, pl.multiple_of(core * half, half))


def gather_kernel(ves_ref, parent_ref, up_ref, out_ref, inflow_ref, *refs):
    *cont_refs, joined = refs
    solutes, cols = out_ref.shape
    joined[:, 0:cols] = up_ref[...]
    joined[:, cols : 2 * cols] = out_ref[...]
    first = ves_ref[0] * cols
    tiles = cols // LANES

    def body(j, carry):
        here = at(j, LANES)
        parent = jnp.broadcast_to(parent_ref[0:1, here], (solutes, LANES))
        seg = first + j * LANES + lax.broadcasted_iota(jnp.int32, (solutes, LANES), 1)
        place = parent - (first - cols)
        lane = lax.bitwise_and(place, LANES - 1)
        tile = lax.shift_right_arithmetic(place, 7) - j
        acc = inflow_ref[:, here]
        tile = jnp.where(parent == seg, -1, tile)
        for t in range(tiles + 1):
            got = jnp.take_along_axis(joined[:, at(j + t, LANES)], lane, axis=1)
            acc = jnp.where(tile == t, got, acc)
        for cont_ref in cont_refs:
            cont_ref[:, here] = acc
        return carry

    lax.fori_loop(0, tiles, body, 0)


def update_kernel(
    total_pts, total_segs, core_ref, a_ref, b_ref, own_ref, got_ref, src_ref, cont_ref, cond_ref,
    par_ref, base_ref, new_ref, *base_out
):
    half = new_ref.shape[1]
    rows = own_ref.shape[1] - LANES
    core = core_ref[0]
    dp = par_ref[2]
    for p in range(half // LANES):
        here = slice(p * LANES, (p + 1) * LANES)
        there = at(core * (half // LANES) + p, LANES)
        wall = (a_ref[:, here] + b_ref[:, here]) / dp
        new_ref[:, here] = RELAX * src_ref[:, there] + RELAX * cond_ref[:, there] * (
            cont_ref[:, there] - wall
        )
    if base_out:
        sink_total = a_ref[:, half : half + LANES] + b_ref[:, half : half + LANES]
        source_total = own_ref[:, rows : rows + LANES] + got_ref[:, rows : rows + LANES]
        base_out[0][...] = base_ref[...] + BALANCE * (
            source_total / total_segs - sink_total / total_pts
        )


def body(
    point_xyz,
    point_cell,
    seg_xyz,
    seg_radius,
    conductance,
    flow_inv,
    parent,
    inflow,
    rate_table,
    half_sat,
    diffusivity,
    base_level,
    sources,
    contents,
):
    pts = point_xyz.shape[1]
    cols = seg_xyz.shape[1]
    solutes = sources.shape[0]
    n_tis = lax.axis_size("tis")
    n_ves = lax.axis_size("ves")
    total_pts = pts * n_tis
    total_segs = cols * n_ves
    rows = pts // PARTS
    half = cols // 2
    tis = lax.axis_index("tis")
    core = (tis % 2).astype(jnp.int32).reshape(1)
    ves = lax.axis_index("ves").astype(jnp.int32).reshape(1)

    def swap(value, bit):
        return lax.ppermute(value, "tis", [(i, i ^ bit) for i in range(n_tis)])

    def from_behind(value):
        return lax.ppermute(value, "ves", [(i, i + 1) for i in range(n_ves - 1)])

    def across(value):
        if n_ves == 2:
            return value, lax.ppermute(value, "ves", [(0, 1), (1, 0)])
        return lax.psum(value, "ves"), jnp.zeros_like(value)

    cond = conductance.reshape(1, cols)
    flow = flow_inv.reshape(1, cols)
    par_row = parent.reshape(1, cols)

    chunk = rows // CHUNKS
    pieces = [[None] * CHUNKS for _ in range(PARTS)]
    level = None
    for sweep in range(ITERS):
        last = sweep == ITERS - 1
        own, got = [], []
        for part in range(PARTS):
            if sweep == 0:
                ins = [
                    ("h", point_xyz), ("h", seg_xyz), ("h", seg_radius.reshape(1, cols)),
                    ("h", sources),
                ]
                outs = [pltpu.VMEM((chunk, cols), BF16)] * CHUNKS + [
                    shape(solutes, rows + (LANES if part == 0 else 0))
                ]
                if part == 0:
                    ins = [("s", core), ("s", ves)] + ins + [
                        ("h", rate_table), ("h", point_cell.reshape(1, pts)), ("hs", half_sat),
                        ("hs", diffusivity), ("hs", base_level), ("h", contents), ("h", flow),
                    ]
                    outs += [
                        shape(solutes, pts), shape(3, solutes, LANES), shape(solutes, LANES),
                        shape(solutes, cols),
                    ]
                else:
                    ins += [("v", t)]
                *made, = call(
                    functools.partial(
                        build_kernel, part, float(total_pts), float(total_segs), CHUNKS
                    ),
                    outs,
                    ins,
                    f"build{part}",
                    scratch=[
                        pltpu.VMEM((3, min(BUILD_ROWS, chunk), LANES), F32),
                        pltpu.VMEM((1, cols), F32), pltpu.VMEM((solutes, cols), BF16),
                    ],
                    limit=BUILD_LIMIT,
                    flops=10 * rows * cols,
                    bytes_accessed=40_000_000,
                )
                pieces[part], t, more = made[:CHUNKS], made[CHUNKS], made[CHUNKS + 1 :]
                if part == 0:
                    rates, par, base, outflow = more
                    upstream = from_behind(outflow)
            else:
                outs = [shape(solutes, rows + (LANES if part == 0 else 0))]
                ins = [("k", piece) for piece in pieces[part]]
                if part == 0:
                    outs += [shape(solutes, cols)] * 2
                    ins += [
                        ("s", core), ("v", new), ("v", theirs), ("v", contents), ("v", flow)
                    ]
                else:
                    ins += [("v", sources)]
                t, *more = call(
                    functools.partial(tissue_kernel, part, CHUNKS),
                    outs,
                    ins,
                    f"tissue{part}",
                    limit=18,
                    scratch=[pltpu.VMEM((solutes, cols), BF16)],
                    flops=2 * solutes * rows * cols,
                    bytes_accessed=10_000_000,
                )
                if part == 0:
                    sources, outflow = more
                    upstream = from_behind(outflow)
            mine, other = across(t)
            own.append(mine)
            got.append(other)

        def wall_ins(part):
            return [("k", piece) for piece in pieces[part]] + [
                ("v", own[part]), ("v", got[part]), ("v", rates), ("v", par), ("v", base),
            ]

        wall, level = call(
            functools.partial(wall_kernel, CHUNKS),
            [shape(solutes, cols + LANES), shape(solutes, rows)],
            wall_ins(0),
            "wall0",
            limit=18,
            scratch=[pltpu.VMEM((solutes, rows), BF16)],
            flops=2 * solutes * rows * cols,
            bytes_accessed=10_000_000,
        )
        send, sink, *more = call(
            functools.partial(send_kernel, last, CHUNKS),
            [shape(solutes, half + LANES), jax.ShapeDtypeStruct((solutes, rows), BF16)]
            + ([shape(solutes, pts)] if last else []),
            wall_ins(1) + [("s", core), ("v", wall), ("v", level), ("v", upstream)],
            "send",
            limit=18,
            flops=solutes * rows * cols,
            bytes_accessed=5_000_000,
        )
        theirs = swap(send, 1)
        (keep,) = call(
            functools.partial(keep_kernel, CHUNKS),
            [shape(solutes, half + LANES)],
            [("k", piece) for piece in pieces[1]]
            + [("s", core), ("v", wall), ("v", send), ("v", sink)],
            "keep",
            limit=18,
            flops=solutes * rows * cols,
            bytes_accessed=5_000_000,
        )
        if last:
            level = more[0]
        new_contents, *copy = call(
            gather_kernel,
            [shape(solutes, cols)] * (2 if last else 1),
            [("s", ves), ("v", par_row), ("v", upstream), ("v", outflow), ("v", inflow)],
            "gather",
            scratch=[pltpu.VMEM((solutes, 2 * cols), F32)],
            flops=solutes * cols * 33,
            bytes_accessed=8_000_000,
        )
        bit = 2
        while bit < n_tis:
            keep = keep + theirs
            theirs = swap(keep, bit)
            bit *= 2
        new, *rest = call(
            functools.partial(update_kernel, float(total_pts), float(total_segs)),
            [shape(solutes, half)] + ([] if last else [shape(solutes, LANES)]),
            [
                ("s", core), ("v", keep), ("v", theirs), ("v", own[0]), ("v", got[0]),
                ("v", sources), ("v", new_contents), ("v", cond), ("v", par), ("v", base),
            ],
            "update",
        )
        base = base if last else rest[0]
        contents = copy[0] if last else new_contents
        theirs = swap(new, 1)
    (sources,) = call(
        join_kernel,
        [shape(solutes, cols)],
        [("s", core), ("v", new), ("v", theirs)],
        "join",
    )
    return (level, sources, contents)


def solution(mesh):
    return jax.shard_map(
        body,
        mesh=mesh,
        in_specs=(
            P(None, "tis"),
            P("tis"),
            P(None, "ves"),
            P("ves"),
            P("ves"),
            P("ves"),
            P("ves"),
            P(None, "ves"),
            P(),
            P(),
            P(),
            P(),
            P(None, "ves"),
            P(None, "ves"),
        ),
        out_specs=(P(None, "tis"), P(None, "ves"), P(None, "ves")),
        check_vma=False,
    )
```

```python
import functools

import jax
import jax.numpy as jnp
from jax import lax
from jax.experimental import pallas as pl
from jax.experimental.pallas import tpu as pltpu
from jax.sharding import PartitionSpec as P

ITERS = 3

RELAX = 0.5
BALANCE = 0.5
LANES = 128
PARTS = 2
CHUNKS = 2
BUILD_ROWS = 128
BUILD_LIMIT = 21


VM = pl.BlockSpec(memory_space=pltpu.VMEM)
SM = pl.BlockSpec(memory_space=pltpu.SMEM)
F32 = jnp.float32
BF16 = jnp.bfloat16


def call(kernel, outs, ins, name, scratch=(), limit=4, flops=0, bytes_accessed=0):
    specs = [SM if space in ("s", "hs") else VM for space, _ in ins]
    pinned = {"k": pltpu.VMEM, "h": pltpu.HBM, "hs": pltpu.HBM}
    arrays = [
        pltpu.with_memory_space_constraint(value, pinned[space]) if space in pinned else value
        for space, value in ins
    ]
    return pl.pallas_call(
        kernel,
        out_shape=tuple(outs),
        in_specs=specs,
        out_specs=(VM,) * len(outs),
        scratch_shapes=list(scratch),
        compiler_params=pltpu.CompilerParams(vmem_limit_bytes=limit << 20),
        cost_estimate=pl.CostEstimate(
            flops=flops, bytes_accessed=bytes_accessed, transcendentals=0
        ),
        name=name,
    )(*arrays)


def shape(*dims):
    return jax.ShapeDtypeStruct(dims, F32)


def at(block, size):
    return pl.ds(pl.multiple_of(block * size, size), size)


def lane_sum(ref, solutes, cols):
    acc = ref[:, 0:LANES]
    for tile in range(1, cols // LANES):
        acc = acc + ref[:, tile * LANES : (tile + 1) * LANES]
    return jnp.broadcast_to(jnp.sum(acc, axis=1, keepdims=True), (solutes, LANES))


def prepare(
    total_pts, total_segs, table_ref, cell_ref, hs_ref, diff_ref, base_ref, cont_ref, flow_ref,
    src_ref, rates_ref, par_ref, base_out, out_ref
):
    solutes, pts = rates_ref.shape
    row = lax.broadcasted_iota(jnp.int32, (solutes, LANES), 0)

    def spread(ref):
        acc = jnp.full((solutes, LANES), ref[0], F32)
        for s in range(1, solutes):
            acc = jnp.where(row == s, ref[s], acc)
        return acc

    diff = spread(diff_ref)
    par_ref[0] = spread(hs_ref)
    par_ref[1] = diff * total_segs
    par_ref[2] = diff * total_pts
    base_out[...] = spread(base_ref)
    out_ref[...] = cont_ref[...] - src_ref[...] * flow_ref[...]
    n_cells = table_ref.shape[1]
    tiles = pl.cdiv(n_cells, LANES)
    spare = tiles * LANES - n_cells
    table = table_ref[...]
    if spare:
        table = jnp.concatenate([table, jnp.zeros((solutes, spare), F32)], axis=1)
    for p in range(pts // LANES):
        cols = slice(p * LANES, (p + 1) * LANES)
        cell = jnp.broadcast_to(cell_ref[0:1, cols], (solutes, LANES))
        lane = lax.bitwise_and(cell, LANES - 1)
        acc = jnp.take_along_axis(table[:, 0:LANES], lane, axis=1)
        for t in range(1, tiles):
            got = jnp.take_along_axis(table[:, t * LANES : (t + 1) * LANES], lane, axis=1)
            acc = jnp.where(lax.shift_right_logical(cell, 7) == t, got, acc)
        rates_ref[:, cols] = acc


def build_kernel(part, total_pts, total_segs, n_k, *refs):
    if part == 0:
        core_ref, ves_ref, pts_ref, seg_ref, rad_ref, src_ref, *refs = refs
        ins, refs = refs[:7], refs[7:]
        k_refs, refs = refs[:n_k], refs[n_k:]
        t_ref, rates_ref, par_ref, base_out, out_ref, pb, rr, sb = refs
        prepare(total_pts, total_segs, *ins, src_ref, rates_ref, par_ref, base_out, out_ref)
    else:
        pts_ref, seg_ref, rad_ref, src_ref, before_ref, *refs = refs
        k_refs, refs = refs[:n_k], refs[n_k:]
        t_ref, pb, rr, sb = refs
    rows, cols = k_refs[0].shape
    whole = n_k * rows
    solutes = src_ref.shape[0]
    rb = min(BUILD_ROWS, rows)
    pc = cols
    rg = 16
    n_pc = cols // pc
    n_rb = rows // rb
    rr[...] = rad_ref[...] * rad_ref[...]
    sb[...] = src_ref[...].astype(BF16)

    def load_points(block):
        p = pts_ref[:, pl.ds(pl.multiple_of(part * whole + block * rb, rb), rb)]
        p = jnp.concatenate([p, jnp.zeros((5, rb), F32)], axis=0)
        pt = jnp.transpose(p)
        for q in range(3):
            pb[q] = jnp.broadcast_to(pt[:, q : q + 1], (rb, LANES))

    def tiles(k_ref, where, points, first, count):
        px, py, pz = points
        for t in range(0, count, 2):
            pair = []
            for u in (0, 1):
                here = slice(first + (t + u) * LANES, first + (t + u + 1) * LANES)
                dx = px - seg_ref[0:1, here]
                dy = py - seg_ref[1:2, here]
                dz = pz - seg_ref[2:3, here]
                pair.append(lax.rsqrt(((dx * dx + dy * dy) + dz * dz) + rr[:, here]))
            both = slice(first + t * LANES, first + (t + 2) * LANES)
            k_ref[where, both] = jnp.concatenate(pair, axis=1).astype(BF16)

    def make(i, r, c):
        for g in range(rb // rg):
            where = pl.ds(pl.multiple_of(r * rb + g * rg, rg), rg)
            points = [pb[q, g * rg : (g + 1) * rg, :] for q in range(3)]
            tiles(k_refs[i], where, points, c * pc, pc // LANES)

    def multiply(i, r, c):
        piece = slice(c * pc, (c + 1) * pc)
        return lax.dot_general(
            sb[:, piece], k_refs[i][at(r, rb), piece], (((1,), (1,)), ((), ())),
            preferred_element_type=F32,
        )

    def step(done, made):
        acc = None
        for c in range(n_pc):
            got = multiply(*done, c)
            acc = got if acc is None else acc + got
            if made is not None:
                make(*made, c)
        t_ref[:, pl.ds(pl.multiple_of(done[0] * rows + done[1] * rb, rb), rb)] = acc

    load_points(0)

    def first(g, carry):
        where = at(g, rg)
        tiles(k_refs[0], where, [pb[q, where, :] for q in range(3)], 0, cols // LANES)
        return carry

    lax.fori_loop(0, rb // rg, first, 0)
    for i in range(n_k):
        if i:
            load_points(i * n_rb)
            step((i - 1, n_rb - 1), (i, 0))

        def body(r, carry):
            load_points(i * n_rb + r)
            step((i, r - 1), (i, r))
            return carry

        lax.fori_loop(1, n_rb, body, 0)
    step((n_k - 1, n_rb - 1), None)
    if part == 0:
        t_ref[:, whole : whole + LANES] = lane_sum(src_ref, solutes, cols)


def add_tissue(t_ref, before_ref, sb, k_refs, first):
    rows = k_refs[0].shape[0]
    width = sb.shape[1]
    rb = min(1024, rows)
    pc = min(1024, width)
    for i, k_ref in enumerate(k_refs):
        for r in range(rows // rb):
            here = slice(i * rows + r * rb, i * rows + (r + 1) * rb)
            acc = None if before_ref is None else before_ref[:, here]
            for c in range(width // pc):
                got = lax.dot_general(
                    sb[:, c * pc : (c + 1) * pc],
                    k_ref[r * rb : (r + 1) * rb, pl.ds(first + c * pc, pc)],
                    (((1,), (1,)), ((), ())),
                    preferred_element_type=F32,
                )
                acc = got if acc is None else acc + got
            t_ref[:, here] = acc


def early_kernel(n_k, *refs):
    k_refs, refs = refs[:n_k], refs[n_k:]
    core_ref, mine_ref, t_ref, sb = refs
    half = mine_ref.shape[1]
    sb[...] = mine_ref[...].astype(BF16)
    add_tissue(t_ref, None, sb, k_refs, pl.multiple_of(core_ref[0] * half, half))


def tissue_kernel(part, n_k, *refs):
    k_refs, refs = refs[:n_k], refs[n_k:]
    solutes = refs[-1].shape[0]
    if part == 0:
        (
            core_ref, mine_ref, theirs_ref, cont_ref, flow_ref, early_ref, t_ref, src_ref, out_ref,
            sb,
        ) = refs
        half = mine_ref.shape[1]
        sb[...] = theirs_ref[...].astype(BF16)
        other = pl.multiple_of((1 - core_ref[0]) * half, half)
        add_tissue(t_ref, early_ref, sb, k_refs, other)
        join_kernel(core_ref, mine_ref, theirs_ref, src_ref)
        out_ref[...] = cont_ref[...] - src_ref[...] * flow_ref[...]
        whole = n_k * k_refs[0].shape[0]
        t_ref[:, whole : whole + LANES] = lane_sum(src_ref, solutes, src_ref.shape[1])
    else:
        src_ref, t_ref, sb = refs
        sb[...] = src_ref[...].astype(BF16)
        add_tissue(t_ref, None, sb, k_refs, 0)


def join_kernel(core_ref, mine_ref, theirs_ref, src_ref):
    half = mine_ref.shape[1]
    core = core_ref[0]
    src_ref[:, at(core, half)] = mine_ref[...]
    src_ref[:, at(1 - core, half)] = theirs_ref[...]


def finish_kernel(
    core_ref, mine_ref, theirs_ref, cont_ref, level_a, level_b, level_ref, src_ref, cont_out
):
    rows = level_a.shape[1]
    join_kernel(core_ref, mine_ref, theirs_ref, src_ref)
    cont_out[...] = cont_ref[...]
    level_ref[:, 0:rows] = level_a[...]
    level_ref[:, rows : 2 * rows] = level_b[...]


def sinks(part, own_refs, got_refs, rates_ref, par_ref, base_ref, tmp, level_ref, first):
    whole = tmp.shape[1]
    solutes = rates_ref.shape[0]
    hs, dn, base = par_ref[0], par_ref[1], base_ref[...]
    total = jnp.zeros((solutes, LANES), F32)
    for p in range(0, whole, LANES):
        here = slice(p, p + LANES)
        level = base + (own_refs[:, here] + got_refs[:, here]) / dn
        rate = rates_ref[:, part * whole + p : part * whole + p + LANES]
        sink = rate * level / (jnp.abs(level) + hs)
        total = total + sink
        tmp[:, here] = sink.astype(BF16)
        if level_ref is not None:
            level_ref[:, first + p : first + p + LANES] = level
    return jnp.broadcast_to(jnp.sum(total, axis=1, keepdims=True), (solutes, LANES))


def add_wall(acc_ref, tmp, k_refs, first):
    width = acc_ref.shape[1] - LANES
    rows = k_refs[0].shape[0]
    for i, k_ref in enumerate(k_refs):
        acc_ref[:, 0:width] += jnp.dot(
            tmp[:, i * rows : (i + 1) * rows], k_ref[:, pl.ds(first, width)],
            preferred_element_type=F32,
        )


def wall_kernel(n_k, *refs):
    k_refs, refs = refs[:n_k], refs[n_k:]
    own_ref, got_ref, rates_ref, par_ref, base_ref, wall_ref, level_ref, tmp = refs
    solutes, cols = rates_ref.shape[0], k_refs[0].shape[1]
    total = sinks(0, own_ref, got_ref, rates_ref, par_ref, base_ref, tmp, level_ref, 0)
    wall_ref[:, 0:cols] = jnp.zeros((solutes, cols), F32)
    wall_ref[:, cols : cols + LANES] = total
    add_wall(wall_ref, tmp, k_refs, 0)


def send_kernel(last, n_k, *refs):
    k_refs, refs = refs[:n_k], refs[n_k:]
    (
        own_ref, got_ref, rates_ref, par_ref, base_ref, core_ref, before_ref, up_ref,
        send_ref, tmp, *more,
    ) = refs
    cols = k_refs[0].shape[1]
    whole = tmp.shape[1]
    half = cols // 2
    level_ref = more[0] if last else None
    total = sinks(1, own_ref, got_ref, rates_ref, par_ref, base_ref, tmp, level_ref, 0)
    other = 1 - core_ref[0]
    send_ref[:, 0:half] = before_ref[:, at(other, half)]
    send_ref[:, half : half + LANES] = before_ref[:, cols : cols + LANES] + total
    add_wall(send_ref, tmp, k_refs, pl.multiple_of(other * half, half))


def keep_kernel(n_k, *refs):
    k_refs, refs = refs[:n_k], refs[n_k:]
    core_ref, before_ref, send_ref, tmp, keep_ref = refs
    half = k_refs[0].shape[1] // 2
    core = core_ref[0]
    keep_ref[:, 0:half] = before_ref[:, at(core, half)]
    keep_ref[:, half : half + LANES] = send_ref[:, half : half + LANES]
    add_wall(keep_ref, tmp, k_refs, pl.multiple_of(core * half, half))


def gather_kernel(ves_ref, parent_ref, up_ref, out_ref, inflow_ref, cont_ref, joined):
    solutes, cols = out_ref.shape
    joined[:, 0:cols] = up_ref[...]
    joined[:, cols : 2 * cols] = out_ref[...]
    first = ves_ref[0] * cols
    tiles = cols // LANES

    def body(j, carry):
        here = at(j, LANES)
        parent = jnp.broadcast_to(parent_ref[0:1, here], (solutes, LANES))
        seg = first + j * LANES + lax.broadcasted_iota(jnp.int32, (solutes, LANES), 1)
        place = parent - (first - cols)
        lane = lax.bitwise_and(place, LANES - 1)
        tile = lax.shift_right_arithmetic(place, 7) - j
        acc = inflow_ref[:, here]
        tile = jnp.where(parent == seg, -1, tile)
        for t in range(tiles + 1):
            got = jnp.take_along_axis(joined[:, at(j + t, LANES)], lane, axis=1)
            acc = jnp.where(tile == t, got, acc)
        cont_ref[:, here] = acc
        return carry

    lax.fori_loop(0, tiles, body, 0)


def update_kernel(
    total_pts, total_segs, core_ref, a_ref, b_ref, own_ref, got_ref, src_ref, cont_ref, cond_ref,
    par_ref, base_ref, new_ref, *base_out
):
    half = new_ref.shape[1]
    rows = own_ref.shape[1] - LANES
    core = core_ref[0]
    dp = par_ref[2]
    for p in range(half // LANES):
        here = slice(p * LANES, (p + 1) * LANES)
        there = at(core * (half // LANES) + p, LANES)
        wall = (a_ref[:, here] + b_ref[:, here]) / dp
        new_ref[:, here] = RELAX * src_ref[:, there] + RELAX * cond_ref[:, there] * (
            cont_ref[:, there] - wall
        )
    if base_out:
        sink_total = a_ref[:, half : half + LANES] + b_ref[:, half : half + LANES]
        source_total = own_ref[:, rows : rows + LANES] + got_ref[:, rows : rows + LANES]
        base_out[0][...] = base_ref[...] + BALANCE * (
            source_total / total_segs - sink_total / total_pts
        )


def body(
    point_xyz,
    point_cell,
    seg_xyz,
    seg_radius,
    conductance,
    flow_inv,
    parent,
    inflow,
    rate_table,
    half_sat,
    diffusivity,
    base_level,
    sources,
    contents,
):
    pts = point_xyz.shape[1]
    cols = seg_xyz.shape[1]
    solutes = sources.shape[0]
    n_tis = lax.axis_size("tis")
    n_ves = lax.axis_size("ves")
    total_pts = pts * n_tis
    total_segs = cols * n_ves
    rows = pts // PARTS
    half = cols // 2
    tis = lax.axis_index("tis")
    core = (tis % 2).astype(jnp.int32).reshape(1)
    ves = lax.axis_index("ves").astype(jnp.int32).reshape(1)

    def swap(value, bit):
        return lax.ppermute(value, "tis", [(i, i ^ bit) for i in range(n_tis)])

    def from_behind(value):
        return lax.ppermute(value, "ves", [(i, i + 1) for i in range(n_ves - 1)])

    def across(value):
        if n_ves == 2:
            return value, lax.ppermute(value, "ves", [(0, 1), (1, 0)])
        return lax.psum(value, "ves"), jnp.zeros_like(value)

    cond = conductance.reshape(1, cols)
    flow = flow_inv.reshape(1, cols)
    par_row = parent.reshape(1, cols)

    chunk = rows // CHUNKS
    pieces = [[None] * CHUNKS for _ in range(PARTS)]
    level = None
    for sweep in range(ITERS):
        last = sweep == ITERS - 1
        own, got = [], []
        for part in range(PARTS):
            if sweep == 0:
                ins = [
                    ("h", point_xyz), ("h", seg_xyz), ("h", seg_radius.reshape(1, cols)),
                    ("h", sources),
                ]
                outs = [pltpu.VMEM((chunk, cols), BF16)] * CHUNKS + [
                    shape(solutes, rows + (LANES if part == 0 else 0))
                ]
                if part == 0:
                    ins = [("s", core), ("s", ves)] + ins + [
                        ("h", rate_table), ("h", point_cell.reshape(1, pts)), ("hs", half_sat),
                        ("hs", diffusivity), ("hs", base_level), ("h", contents), ("h", flow),
                    ]
                    outs += [
                        shape(solutes, pts), shape(3, solutes, LANES), shape(solutes, LANES),
                        shape(solutes, cols),
                    ]
                else:
                    ins += [("v", t)]
                *made, = call(
                    functools.partial(
                        build_kernel, part, float(total_pts), float(total_segs), CHUNKS
                    ),
                    outs,
                    ins,
                    f"build{part}",
                    scratch=[
                        pltpu.VMEM((3, min(BUILD_ROWS, chunk), LANES), F32),
                        pltpu.VMEM((1, cols), F32), pltpu.VMEM((solutes, cols), BF16),
                    ],
                    limit=BUILD_LIMIT,
                    flops=10 * rows * cols,
                    bytes_accessed=40_000_000,
                )
                pieces[part], t, more = made[:CHUNKS], made[CHUNKS], made[CHUNKS + 1 :]
                if part == 0:
                    rates, par, base, outflow = more
                    upstream = from_behind(outflow)
            else:
                outs = [shape(solutes, rows + (LANES if part == 0 else 0))]
                ins = [("k", piece) for piece in pieces[part]]
                if part == 0:
                    outs += [shape(solutes, cols)] * 2
                    ins += [
                        ("s", core), ("v", new), ("v", theirs), ("v", contents), ("v", flow),
                        ("v", early),
                    ]
                else:
                    ins += [("v", sources)]
                t, *more = call(
                    functools.partial(tissue_kernel, part, CHUNKS),
                    outs,
                    ins,
                    f"tissue{part}",
                    limit=18,
                    scratch=[pltpu.VMEM((solutes, half if part == 0 else cols), BF16)],
                    flops=2 * solutes * rows * cols,
                    bytes_accessed=10_000_000,
                )
                if part == 0:
                    sources, outflow = more
                    upstream = from_behind(outflow)
            mine, other = across(t)
            own.append(mine)
            got.append(other)

        def wall_ins(part):
            return [("k", piece) for piece in pieces[part]] + [
                ("v", own[part]), ("v", got[part]), ("v", rates), ("v", par), ("v", base),
            ]

        wall, level = call(
            functools.partial(wall_kernel, CHUNKS),
            [shape(solutes, cols + LANES), shape(solutes, rows)],
            wall_ins(0),
            "wall0",
            limit=18,
            scratch=[pltpu.VMEM((solutes, rows), BF16)],
            flops=2 * solutes * rows * cols,
            bytes_accessed=10_000_000,
        )
        send, sink, *more = call(
            functools.partial(send_kernel, last, CHUNKS),
            [shape(solutes, half + LANES), jax.ShapeDtypeStruct((solutes, rows), BF16)]
            + ([shape(solutes, rows)] if last else []),
            wall_ins(1) + [("s", core), ("v", wall), ("v", upstream)],
            "send",
            limit=18,
            flops=solutes * rows * cols,
            bytes_accessed=5_000_000,
        )
        theirs = swap(send, 1)
        (keep,) = call(
            functools.partial(keep_kernel, CHUNKS),
            [shape(solutes, half + LANES)],
            [("k", piece) for piece in pieces[1]]
            + [("s", core), ("v", wall), ("v", send), ("v", sink)],
            "keep",
            limit=18,
            flops=solutes * rows * cols,
            bytes_accessed=5_000_000,
        )
        if last:
            levels = (level, more[0])
        (new_contents,) = call(
            gather_kernel,
            [shape(solutes, cols)],
            [("s", ves), ("v", par_row), ("v", upstream), ("v", outflow), ("v", inflow)],
            "gather",
            scratch=[pltpu.VMEM((solutes, 2 * cols), F32)],
            flops=solutes * cols * 33,
            bytes_accessed=8_000_000,
        )
        bit = 2
        while bit < n_tis:
            keep = keep + theirs
            theirs = swap(keep, bit)
            bit *= 2
        new, *rest = call(
            functools.partial(update_kernel, float(total_pts), float(total_segs)),
            [shape(solutes, half)] + ([] if last else [shape(solutes, LANES)]),
            [
                ("s", core), ("v", keep), ("v", theirs), ("v", own[0]), ("v", got[0]),
                ("v", sources), ("v", new_contents), ("v", cond), ("v", par), ("v", base),
            ],
            "update",
        )
        base = base if last else rest[0]
        contents = new_contents
        theirs = swap(new, 1)
        if not last:
            (early,) = call(
                functools.partial(early_kernel, CHUNKS),
                [shape(solutes, rows)],
                [("k", piece) for piece in pieces[0]] + [("s", core), ("v", new)],
                "early",
                limit=18,
                scratch=[pltpu.VMEM((solutes, half), BF16)],
                flops=solutes * rows * cols,
                bytes_accessed=5_000_000,
            )
    return call(
        finish_kernel,
        [shape(solutes, pts), shape(solutes, cols), shape(solutes, cols)],
        [("s", core), ("v", new), ("v", theirs), ("v", contents)] + [("v", x) for x in levels],
        "finish",
    )


def solution(mesh):
    return jax.shard_map(
        body,
        mesh=mesh,
        in_specs=(
            P(None, "tis"),
            P("tis"),
            P(None, "ves"),
            P("ves"),
            P("ves"),
            P("ves"),
            P("ves"),
            P(None, "ves"),
            P(),
            P(),
            P(),
            P(),
            P(None, "ves"),
            P(None, "ves"),
        ),
        out_specs=(P(None, "tis"), P(None, "ves"), P(None, "ves")),
        check_vma=False,
    )
```

```python
import functools

import jax
import jax.numpy as jnp
from jax import lax
from jax.experimental import pallas as pl
from jax.experimental.pallas import tpu as pltpu
from jax.sharding import PartitionSpec as P

ITERS = 3

RELAX = 0.5
BALANCE = 0.5
LANES = 128
PARTS = 2
CHUNKS = 2
BUILD_ROWS = 128
BUILD_LIMIT = 21


VM = pl.BlockSpec(memory_space=pltpu.VMEM)
SM = pl.BlockSpec(memory_space=pltpu.SMEM)
F32 = jnp.float32
BF16 = jnp.bfloat16


def call(kernel, outs, ins, name, scratch=(), limit=4, flops=0, bytes_accessed=0):
    specs = [SM if space in ("s", "hs") else VM for space, _ in ins]
    pinned = {"k": pltpu.VMEM, "h": pltpu.HBM, "hs": pltpu.HBM}
    arrays = [
        pltpu.with_memory_space_constraint(value, pinned[space]) if space in pinned else value
        for space, value in ins
    ]
    return pl.pallas_call(
        kernel,
        out_shape=tuple(outs),
        in_specs=specs,
        out_specs=(VM,) * len(outs),
        scratch_shapes=list(scratch),
        compiler_params=pltpu.CompilerParams(vmem_limit_bytes=limit << 20),
        cost_estimate=pl.CostEstimate(
            flops=flops, bytes_accessed=bytes_accessed, transcendentals=0
        ),
        name=name,
    )(*arrays)


def shape(*dims):
    return jax.ShapeDtypeStruct(dims, F32)


def at(block, size):
    return pl.ds(pl.multiple_of(block * size, size), size)


def lane_sum(ref, solutes, cols):
    acc = ref[:, 0:LANES]
    for tile in range(1, cols // LANES):
        acc = acc + ref[:, tile * LANES : (tile + 1) * LANES]
    return jnp.broadcast_to(jnp.sum(acc, axis=1, keepdims=True), (solutes, LANES))


def prepare(
    total_pts, total_segs, table_ref, cell_ref, hs_ref, diff_ref, base_ref, cont_ref, flow_ref,
    src_ref, rates_ref, par_ref, base_out, out_ref
):
    solutes, pts = rates_ref.shape
    row = lax.broadcasted_iota(jnp.int32, (solutes, LANES), 0)

    def spread(ref):
        acc = jnp.full((solutes, LANES), ref[0], F32)
        for s in range(1, solutes):
            acc = jnp.where(row == s, ref[s], acc)
        return acc

    diff = spread(diff_ref)
    par_ref[0] = spread(hs_ref)
    par_ref[1] = diff * total_segs
    par_ref[2] = diff * total_pts
    base_out[...] = spread(base_ref)
    out_ref[...] = cont_ref[...] - src_ref[...] * flow_ref[...]
    n_cells = table_ref.shape[1]
    tiles = pl.cdiv(n_cells, LANES)
    spare = tiles * LANES - n_cells
    table = table_ref[...]
    if spare:
        table = jnp.concatenate([table, jnp.zeros((solutes, spare), F32)], axis=1)
    for p in range(pts // LANES):
        cols = slice(p * LANES, (p + 1) * LANES)
        cell = jnp.broadcast_to(cell_ref[0:1, cols], (solutes, LANES))
        lane = lax.bitwise_and(cell, LANES - 1)
        acc = jnp.take_along_axis(table[:, 0:LANES], lane, axis=1)
        for t in range(1, tiles):
            got = jnp.take_along_axis(table[:, t * LANES : (t + 1) * LANES], lane, axis=1)
            acc = jnp.where(lax.shift_right_logical(cell, 7) == t, got, acc)
        rates_ref[:, cols] = acc


def build_kernel(part, total_pts, total_segs, n_k, *refs):
    if part == 0:
        core_ref, ves_ref, pts_ref, seg_ref, rad_ref, src_ref, *refs = refs
        ins, refs = refs[:7], refs[7:]
        k_refs, refs = refs[:n_k], refs[n_k:]
        t_ref, rates_ref, par_ref, base_out, out_ref, pb, rr, sb = refs
        prepare(total_pts, total_segs, *ins, src_ref, rates_ref, par_ref, base_out, out_ref)
    else:
        pts_ref, seg_ref, rad_ref, src_ref, before_ref, *refs = refs
        k_refs, refs = refs[:n_k], refs[n_k:]
        t_ref, pb, rr, sb = refs
    rows, cols = k_refs[0].shape
    whole = n_k * rows
    solutes = src_ref.shape[0]
    rb = min(BUILD_ROWS, rows)
    pc = cols
    rg = 16
    n_pc = cols // pc
    n_rb = rows // rb
    rr[...] = rad_ref[...] * rad_ref[...]
    sb[...] = src_ref[...].astype(BF16)

    def load_points(block):
        p = pts_ref[:, pl.ds(pl.multiple_of(part * whole + block * rb, rb), rb)]
        p = jnp.concatenate([p, jnp.zeros((5, rb), F32)], axis=0)
        pt = jnp.transpose(p)
        for q in range(3):
            pb[q] = jnp.broadcast_to(pt[:, q : q + 1], (rb, LANES))

    def tiles(k_ref, where, points, first, count):
        px, py, pz = points
        for t in range(0, count, 2):
            pair = []
            for u in (0, 1):
                here = slice(first + (t + u) * LANES, first + (t + u + 1) * LANES)
                dx = px - seg_ref[0:1, here]
                dy = py - seg_ref[1:2, here]
                dz = pz - seg_ref[2:3, here]
                pair.append(lax.rsqrt(((dx * dx + dy * dy) + dz * dz) + rr[:, here]))
            both = slice(first + t * LANES, first + (t + 2) * LANES)
            k_ref[where, both] = jnp.concatenate(pair, axis=1).astype(BF16)

    def make(i, r, c):
        for g in range(rb // rg):
            where = pl.ds(pl.multiple_of(r * rb + g * rg, rg), rg)
            points = [pb[q, g * rg : (g + 1) * rg, :] for q in range(3)]
            tiles(k_refs[i], where, points, c * pc, pc // LANES)

    def multiply(i, r, c):
        piece = slice(c * pc, (c + 1) * pc)
        return lax.dot_general(
            sb[:, piece], k_refs[i][at(r, rb), piece], (((1,), (1,)), ((), ())),
            preferred_element_type=F32,
        )

    def step(done, made):
        acc = None
        for c in range(n_pc):
            got = multiply(*done, c)
            acc = got if acc is None else acc + got
            if made is not None:
                make(*made, c)
        t_ref[:, pl.ds(pl.multiple_of(done[0] * rows + done[1] * rb, rb), rb)] = acc

    load_points(0)

    def first(g, carry):
        where = at(g, rg)
        tiles(k_refs[0], where, [pb[q, where, :] for q in range(3)], 0, cols // LANES)
        return carry

    lax.fori_loop(0, rb // rg, first, 0)
    for i in range(n_k):
        if i:
            load_points(i * n_rb)
            step((i - 1, n_rb - 1), (i, 0))

        def body(r, carry):
            load_points(i * n_rb + r)
            step((i, r - 1), (i, r))
            return carry

        lax.fori_loop(1, n_rb, body, 0)
    step((n_k - 1, n_rb - 1), None)
    if part == 0:
        t_ref[:, whole : whole + LANES] = lane_sum(src_ref, solutes, cols)


def add_tissue(t_ref, before_ref, sb, k_refs, first):
    rows = k_refs[0].shape[0]
    width = sb.shape[1]
    rb = min(1024, rows)
    pc = min(1024, width)
    for i, k_ref in enumerate(k_refs):
        for r in range(rows // rb):
            here = slice(i * rows + r * rb, i * rows + (r + 1) * rb)
            acc = None if before_ref is None else before_ref[:, here]
            for c in range(width // pc):
                got = lax.dot_general(
                    sb[:, c * pc : (c + 1) * pc],
                    k_ref[r * rb : (r + 1) * rb, pl.ds(first + c * pc, pc)],
                    (((1,), (1,)), ((), ())),
                    preferred_element_type=F32,
                )
                acc = got if acc is None else acc + got
            t_ref[:, here] = acc


def early_kernel(n_k, *refs):
    k_refs, refs = refs[:n_k], refs[n_k:]
    core_ref, mine_ref, t_ref, sb = refs
    half = mine_ref.shape[1]
    sb[...] = mine_ref[...].astype(BF16)
    add_tissue(t_ref, None, sb, k_refs, pl.multiple_of(core_ref[0] * half, half))


def tissue_kernel(part, n_k, *refs):
    k_refs, refs = refs[:n_k], refs[n_k:]
    solutes = refs[-1].shape[0]
    if part == 0:
        (
            core_ref, mine_ref, theirs_ref, cont_ref, flow_ref, early_ref, t_ref, src_ref, out_ref,
            sb,
        ) = refs
        half = mine_ref.shape[1]
        sb[...] = theirs_ref[...].astype(BF16)
        other = pl.multiple_of((1 - core_ref[0]) * half, half)
        add_tissue(t_ref, early_ref, sb, k_refs, other)
        join_kernel(core_ref, mine_ref, theirs_ref, src_ref)
        out_ref[...] = cont_ref[...] - src_ref[...] * flow_ref[...]
        whole = n_k * k_refs[0].shape[0]
        t_ref[:, whole : whole + LANES] = lane_sum(src_ref, solutes, src_ref.shape[1])
    else:
        src_ref, t_ref, sb = refs
        sb[...] = src_ref[...].astype(BF16)
        add_tissue(t_ref, None, sb, k_refs, 0)


def join_kernel(core_ref, mine_ref, theirs_ref, src_ref):
    half = mine_ref.shape[1]
    core = core_ref[0]
    src_ref[:, at(core, half)] = mine_ref[...]
    src_ref[:, at(1 - core, half)] = theirs_ref[...]


def finish_kernel(
    core_ref, mine_ref, theirs_ref, cont_ref, level_a, level_b, level_ref, src_ref, cont_out
):
    rows = level_a.shape[1]
    join_kernel(core_ref, mine_ref, theirs_ref, src_ref)
    cont_out[...] = cont_ref[...]
    level_ref[:, 0:rows] = level_a[...]
    level_ref[:, rows : 2 * rows] = level_b[...]


def sinks(part, own_refs, got_refs, rates_ref, par_ref, base_ref, tmp, level_ref, first):
    whole = tmp.shape[1]
    solutes = rates_ref.shape[0]
    hs, dn, base = par_ref[0], par_ref[1], base_ref[...]
    total = jnp.zeros((solutes, LANES), F32)
    for p in range(0, whole, LANES):
        here = slice(p, p + LANES)
        level = base + (own_refs[:, here] + got_refs[:, here]) / dn
        rate = rates_ref[:, part * whole + p : part * whole + p + LANES]
        sink = rate * level / (jnp.abs(level) + hs)
        total = total + sink
        tmp[:, here] = sink.astype(BF16)
        if level_ref is not None:
            level_ref[:, first + p : first + p + LANES] = level
    return jnp.broadcast_to(jnp.sum(total, axis=1, keepdims=True), (solutes, LANES))


def add_wall(acc_ref, tmp, k_refs, first):
    width = acc_ref.shape[1] - LANES
    rows = k_refs[0].shape[0]
    for i, k_ref in enumerate(k_refs):
        acc_ref[:, 0:width] += jnp.dot(
            tmp[:, i * rows : (i + 1) * rows], k_ref[:, pl.ds(first, width)],
            preferred_element_type=F32,
        )


def wall_kernel(n_k, *refs):
    k_refs, refs = refs[:n_k], refs[n_k:]
    own_ref, got_ref, rates_ref, par_ref, base_ref, wall_ref, level_ref, tmp = refs
    solutes, cols = rates_ref.shape[0], k_refs[0].shape[1]
    total = sinks(0, own_ref, got_ref, rates_ref, par_ref, base_ref, tmp, level_ref, 0)
    wall_ref[:, 0:cols] = jnp.zeros((solutes, cols), F32)
    wall_ref[:, cols : cols + LANES] = total
    add_wall(wall_ref, tmp, k_refs, 0)


def send_kernel(last, n_k, *refs):
    k_refs, refs = refs[:n_k], refs[n_k:]
    (
        own_ref, got_ref, rates_ref, par_ref, base_ref, core_ref, before_ref, up_ref,
        send_ref, tmp, *more,
    ) = refs
    cols = k_refs[0].shape[1]
    whole = tmp.shape[1]
    half = cols // 2
    level_ref = more[0] if last else None
    total = sinks(1, own_ref, got_ref, rates_ref, par_ref, base_ref, tmp, level_ref, 0)
    other = 1 - core_ref[0]
    send_ref[:, 0:half] = before_ref[:, at(other, half)]
    send_ref[:, half : half + LANES] = before_ref[:, cols : cols + LANES] + total
    add_wall(send_ref, tmp, k_refs, pl.multiple_of(other * half, half))


def keep_kernel(n_k, *refs):
    k_refs, refs = refs[:n_k], refs[n_k:]
    core_ref, before_ref, send_ref, tmp, keep_ref = refs
    half = k_refs[0].shape[1] // 2
    core = core_ref[0]
    keep_ref[:, 0:half] = before_ref[:, at(core, half)]
    keep_ref[:, half : half + LANES] = send_ref[:, half : half + LANES]
    add_wall(keep_ref, tmp, k_refs, pl.multiple_of(core * half, half))


def gather_kernel(ves_ref, parent_ref, up_ref, out_ref, inflow_ref, cont_ref, joined):
    solutes, cols = out_ref.shape
    joined[:, 0:cols] = up_ref[...]
    joined[:, cols : 2 * cols] = out_ref[...]
    first = ves_ref[0] * cols
    tiles = cols // LANES

    def body(j, carry):
        here = at(j, LANES)
        parent = jnp.broadcast_to(parent_ref[0:1, here], (solutes, LANES))
        seg = first + j * LANES + lax.broadcasted_iota(jnp.int32, (solutes, LANES), 1)
        place = parent - (first - cols)
        lane = lax.bitwise_and(place, LANES - 1)
        tile = lax.shift_right_arithmetic(place, 7) - j
        acc = inflow_ref[:, here]
        tile = jnp.where(parent == seg, -1, tile)
        for t in range(tiles + 1):
            got = jnp.take_along_axis(joined[:, at(j + t, LANES)], lane, axis=1)
            acc = jnp.where(tile == t, got, acc)
        cont_ref[:, here] = acc
        return carry

    lax.fori_loop(0, tiles, body, 0)


def update_kernel(
    total_pts, total_segs, core_ref, a_ref, b_ref, own_ref, got_ref, src_ref, cont_ref, cond_ref,
    par_ref, base_ref, new_ref, *base_out
):
    half = new_ref.shape[1]
    rows = own_ref.shape[1] - LANES
    core = core_ref[0]
    dp = par_ref[2]
    for p in range(half // LANES):
        here = slice(p * LANES, (p + 1) * LANES)
        there = at(core * (half // LANES) + p, LANES)
        wall = (a_ref[:, here] + b_ref[:, here]) / dp
        new_ref[:, here] = RELAX * src_ref[:, there] + RELAX * cond_ref[:, there] * (
            cont_ref[:, there] - wall
        )
    if base_out:
        sink_total = a_ref[:, half : half + LANES] + b_ref[:, half : half + LANES]
        source_total = own_ref[:, rows : rows + LANES] + got_ref[:, rows : rows + LANES]
        base_out[0][...] = base_ref[...] + BALANCE * (
            source_total / total_segs - sink_total / total_pts
        )


def body(
    point_xyz,
    point_cell,
    seg_xyz,
    seg_radius,
    conductance,
    flow_inv,
    parent,
    inflow,
    rate_table,
    half_sat,
    diffusivity,
    base_level,
    sources,
    contents,
):
    pts = point_xyz.shape[1]
    cols = seg_xyz.shape[1]
    solutes = sources.shape[0]
    n_tis = lax.axis_size("tis")
    n_ves = lax.axis_size("ves")
    total_pts = pts * n_tis
    total_segs = cols * n_ves
    rows = pts // PARTS
    half = cols // 2
    tis = lax.axis_index("tis")
    core = (tis % 2).astype(jnp.int32).reshape(1)
    ves = lax.axis_index("ves").astype(jnp.int32).reshape(1)

    def swap(value, bit):
        return lax.ppermute(value, "tis", [(i, i ^ bit) for i in range(n_tis)])

    def from_behind(value):
        return lax.ppermute(value, "ves", [(i, (i + 1) % n_ves) for i in range(n_ves)])

    def across(value):
        if n_ves == 2:
            return value, lax.ppermute(value, "ves", [(0, 1), (1, 0)])
        return lax.psum(value, "ves"), jnp.zeros_like(value)

    cond = conductance.reshape(1, cols)
    flow = flow_inv.reshape(1, cols)
    par_row = parent.reshape(1, cols)

    chunk = rows // CHUNKS
    pieces = [[None] * CHUNKS for _ in range(PARTS)]
    level = None
    for sweep in range(ITERS):
        last = sweep == ITERS - 1
        own, got = [], []
        for part in range(PARTS):
            if sweep == 0:
                ins = [
                    ("h", point_xyz), ("h", seg_xyz), ("h", seg_radius.reshape(1, cols)),
                    ("h", sources),
                ]
                outs = [pltpu.VMEM((chunk, cols), BF16)] * CHUNKS + [
                    shape(solutes, rows + (LANES if part == 0 else 0))
                ]
                if part == 0:
                    ins = [("s", core), ("s", ves)] + ins + [
                        ("h", rate_table), ("h", point_cell.reshape(1, pts)), ("hs", half_sat),
                        ("hs", diffusivity), ("hs", base_level), ("h", contents), ("h", flow),
                    ]
                    outs += [
                        shape(solutes, pts), shape(3, solutes, LANES), shape(solutes, LANES),
                        shape(solutes, cols),
                    ]
                else:
                    ins += [("v", t)]
                *made, = call(
                    functools.partial(
                        build_kernel, part, float(total_pts), float(total_segs), CHUNKS
                    ),
                    outs,
                    ins,
                    f"build{part}",
                    scratch=[
                        pltpu.VMEM((3, min(BUILD_ROWS, chunk), LANES), F32),
                        pltpu.VMEM((1, cols), F32), pltpu.VMEM((solutes, cols), BF16),
                    ],
                    limit=BUILD_LIMIT,
                    flops=10 * rows * cols,
                    bytes_accessed=40_000_000,
                )
                pieces[part], t, more = made[:CHUNKS], made[CHUNKS], made[CHUNKS + 1 :]
                if part == 0:
                    rates, par, base, outflow = more
                    upstream = from_behind(outflow)
            else:
                outs = [shape(solutes, rows + (LANES if part == 0 else 0))]
                ins = [("k", piece) for piece in pieces[part]]
                if part == 0:
                    outs += [shape(solutes, cols)] * 2
                    ins += [
                        ("s", core), ("v", new), ("v", theirs), ("v", contents), ("v", flow),
                        ("v", early),
                    ]
                else:
                    ins += [("v", sources)]
                t, *more = call(
                    functools.partial(tissue_kernel, part, CHUNKS),
                    outs,
                    ins,
                    f"tissue{part}",
                    limit=18,
                    scratch=[pltpu.VMEM((solutes, half if part == 0 else cols), BF16)],
                    flops=2 * solutes * rows * cols,
                    bytes_accessed=10_000_000,
                )
                if part == 0:
                    sources, outflow = more
                    upstream = from_behind(outflow)
            mine, other = across(t)
            own.append(mine)
            got.append(other)

        def wall_ins(part):
            return [("k", piece) for piece in pieces[part]] + [
                ("v", own[part]), ("v", got[part]), ("v", rates), ("v", par), ("v", base),
            ]

        wall, level = call(
            functools.partial(wall_kernel, CHUNKS),
            [shape(solutes, cols + LANES), shape(solutes, rows)],
            wall_ins(0),
            "wall0",
            limit=18,
            scratch=[pltpu.VMEM((solutes, rows), BF16)],
            flops=2 * solutes * rows * cols,
            bytes_accessed=10_000_000,
        )
        send, sink, *more = call(
            functools.partial(send_kernel, last, CHUNKS),
            [shape(solutes, half + LANES), jax.ShapeDtypeStruct((solutes, rows), BF16)]
            + ([shape(solutes, rows)] if last else []),
            wall_ins(1) + [("s", core), ("v", wall), ("v", upstream)],
            "send",
            limit=18,
            flops=solutes * rows * cols,
            bytes_accessed=5_000_000,
        )
        theirs = swap(send, 1)
        (keep,) = call(
            functools.partial(keep_kernel, CHUNKS),
            [shape(solutes, half + LANES)],
            [("k", piece) for piece in pieces[1]]
            + [("s", core), ("v", wall), ("v", send), ("v", sink)],
            "keep",
            limit=18,
            flops=solutes * rows * cols,
            bytes_accessed=5_000_000,
        )
        if last:
            levels = (level, more[0])
        (new_contents,) = call(
            gather_kernel,
            [shape(solutes, cols)],
            [("s", ves), ("v", par_row), ("v", upstream), ("v", outflow), ("v", inflow)],
            "gather",
            scratch=[pltpu.VMEM((solutes, 2 * cols), F32)],
            flops=solutes * cols * 33,
            bytes_accessed=8_000_000,
        )
        bit = 2
        while bit < n_tis:
            keep = keep + theirs
            theirs = swap(keep, bit)
            bit *= 2
        new, *rest = call(
            functools.partial(update_kernel, float(total_pts), float(total_segs)),
            [shape(solutes, half)] + ([] if last else [shape(solutes, LANES)]),
            [
                ("s", core), ("v", keep), ("v", theirs), ("v", own[0]), ("v", got[0]),
                ("v", sources), ("v", new_contents), ("v", cond), ("v", par), ("v", base),
            ],
            "update",
        )
        base = base if last else rest[0]
        contents = new_contents
        theirs = swap(new, 1)
        if not last:
            (early,) = call(
                functools.partial(early_kernel, CHUNKS),
                [shape(solutes, rows)],
                [("k", piece) for piece in pieces[0]] + [("s", core), ("v", new)],
                "early",
                limit=18,
                scratch=[pltpu.VMEM((solutes, half), BF16)],
                flops=solutes * rows * cols,
                bytes_accessed=5_000_000,
            )
    return call(
        finish_kernel,
        [shape(solutes, pts), shape(solutes, cols), shape(solutes, cols)],
        [("s", core), ("v", new), ("v", theirs), ("v", contents)] + [("v", x) for x in levels],
        "finish",
    )


def solution(mesh):
    return jax.shard_map(
        body,
        mesh=mesh,
        in_specs=(
            P(None, "tis"),
            P("tis"),
            P(None, "ves"),
            P("ves"),
            P("ves"),
            P("ves"),
            P("ves"),
            P(None, "ves"),
            P(),
            P(),
            P(),
            P(),
            P(None, "ves"),
            P(None, "ves"),
        ),
        out_specs=(P(None, "tis"), P(None, "ves"), P(None, "ves")),
        check_vma=False,
    )
```

```python
import functools

import jax
import jax.numpy as jnp
from jax import lax
from jax.experimental import pallas as pl
from jax.experimental.pallas import tpu as pltpu
from jax.sharding import PartitionSpec as P

ITERS = 3

RELAX = 0.5
BALANCE = 0.5
LANES = 128
PARTS = 2
CHUNKS = 2
BUILD_ROWS = 128
BUILD_LIMIT = 21


VM = pl.BlockSpec(memory_space=pltpu.VMEM)
SM = pl.BlockSpec(memory_space=pltpu.SMEM)
F32 = jnp.float32
BF16 = jnp.bfloat16


def call(kernel, outs, ins, name, scratch=(), limit=4, flops=0, bytes_accessed=0):
    specs = [SM if space in ("s", "hs") else VM for space, _ in ins]
    pinned = {"k": pltpu.VMEM, "h": pltpu.HBM, "hs": pltpu.HBM}
    arrays = [
        pltpu.with_memory_space_constraint(value, pinned[space]) if space in pinned else value
        for space, value in ins
    ]
    return pl.pallas_call(
        kernel,
        out_shape=tuple(outs),
        in_specs=specs,
        out_specs=(VM,) * len(outs),
        scratch_shapes=list(scratch),
        compiler_params=pltpu.CompilerParams(vmem_limit_bytes=limit << 20),
        cost_estimate=pl.CostEstimate(
            flops=flops, bytes_accessed=bytes_accessed, transcendentals=0
        ),
        name=name,
    )(*arrays)


def shape(*dims):
    return jax.ShapeDtypeStruct(dims, F32)


def at(block, size):
    return pl.ds(pl.multiple_of(block * size, size), size)


def lane_sum(ref, solutes, cols):
    acc = ref[:, 0:LANES]
    for tile in range(1, cols // LANES):
        acc = acc + ref[:, tile * LANES : (tile + 1) * LANES]
    return jnp.broadcast_to(jnp.sum(acc, axis=1, keepdims=True), (solutes, LANES))


def prepare(
    total_pts, total_segs, table_ref, cell_ref, hs_ref, diff_ref, base_ref, cont_ref, flow_ref,
    src_ref, rates_ref, par_ref, base_out, out_ref, first
):
    solutes, pts = rates_ref.shape
    row = lax.broadcasted_iota(jnp.int32, (solutes, LANES), 0)

    def spread(ref):
        acc = jnp.full((solutes, LANES), ref[0], F32)
        for s in range(1, solutes):
            acc = jnp.where(row == s, ref[s], acc)
        return acc

    diff = spread(diff_ref)
    par_ref[0] = spread(hs_ref)
    par_ref[1] = diff * total_segs
    par_ref[2] = diff * total_pts
    base_out[...] = spread(base_ref)
    out_ref[:, first:] = cont_ref[...] - src_ref[...] * flow_ref[...]
    n_cells = table_ref.shape[1]
    tiles = pl.cdiv(n_cells, LANES)
    spare = tiles * LANES - n_cells
    table = table_ref[...]
    if spare:
        table = jnp.concatenate([table, jnp.zeros((solutes, spare), F32)], axis=1)
    for p in range(pts // LANES):
        cols = slice(p * LANES, (p + 1) * LANES)
        cell = jnp.broadcast_to(cell_ref[0:1, cols], (solutes, LANES))
        lane = lax.bitwise_and(cell, LANES - 1)
        acc = jnp.take_along_axis(table[:, 0:LANES], lane, axis=1)
        for t in range(1, tiles):
            got = jnp.take_along_axis(table[:, t * LANES : (t + 1) * LANES], lane, axis=1)
            acc = jnp.where(lax.shift_right_logical(cell, 7) == t, got, acc)
        rates_ref[:, cols] = acc


def build_kernel(part, total_pts, total_segs, n_k, *refs):
    if part == 0:
        core_ref, ves_ref, pts_ref, seg_ref, rad_ref, src_ref, *refs = refs
        ins, refs = refs[:7], refs[7:]
        k_refs, refs = refs[:n_k], refs[n_k:]
        t_ref, rates_ref, par_ref, base_out, pb, rr, sb = refs
        first_out = n_k * k_refs[0].shape[0] + LANES
        prepare(
            total_pts, total_segs, *ins, src_ref, rates_ref, par_ref, base_out, t_ref, first_out
        )
    else:
        pts_ref, seg_ref, rad_ref, src_ref, before_ref, *refs = refs
        k_refs, refs = refs[:n_k], refs[n_k:]
        t_ref, pb, rr, sb = refs
    rows, cols = k_refs[0].shape
    whole = n_k * rows
    solutes = src_ref.shape[0]
    rb = min(BUILD_ROWS, rows)
    pc = cols
    rg = 16
    n_pc = cols // pc
    n_rb = rows // rb
    rr[...] = rad_ref[...] * rad_ref[...]
    sb[...] = src_ref[...].astype(BF16)

    def load_points(block):
        p = pts_ref[:, pl.ds(pl.multiple_of(part * whole + block * rb, rb), rb)]
        p = jnp.concatenate([p, jnp.zeros((5, rb), F32)], axis=0)
        pt = jnp.transpose(p)
        for q in range(3):
            pb[q] = jnp.broadcast_to(pt[:, q : q + 1], (rb, LANES))

    def tiles(k_ref, where, points, first, count):
        px, py, pz = points
        for t in range(0, count, 2):
            pair = []
            for u in (0, 1):
                here = slice(first + (t + u) * LANES, first + (t + u + 1) * LANES)
                dx = px - seg_ref[0:1, here]
                dy = py - seg_ref[1:2, here]
                dz = pz - seg_ref[2:3, here]
                pair.append(lax.rsqrt(((dx * dx + dy * dy) + dz * dz) + rr[:, here]))
            both = slice(first + t * LANES, first + (t + 2) * LANES)
            k_ref[where, both] = jnp.concatenate(pair, axis=1).astype(BF16)

    def make(i, r, c):
        for g in range(rb // rg):
            where = pl.ds(pl.multiple_of(r * rb + g * rg, rg), rg)
            points = [pb[q, g * rg : (g + 1) * rg, :] for q in range(3)]
            tiles(k_refs[i], where, points, c * pc, pc // LANES)

    def multiply(i, r, c):
        piece = slice(c * pc, (c + 1) * pc)
        return lax.dot_general(
            sb[:, piece], k_refs[i][at(r, rb), piece], (((1,), (1,)), ((), ())),
            preferred_element_type=F32,
        )

    def step(done, made):
        acc = None
        for c in range(n_pc):
            got = multiply(*done, c)
            acc = got if acc is None else acc + got
            if made is not None:
                make(*made, c)
        t_ref[:, pl.ds(pl.multiple_of(done[0] * rows + done[1] * rb, rb), rb)] = acc

    load_points(0)

    def first(g, carry):
        where = at(g, rg)
        tiles(k_refs[0], where, [pb[q, where, :] for q in range(3)], 0, cols // LANES)
        return carry

    lax.fori_loop(0, rb // rg, first, 0)
    for i in range(n_k):
        if i:
            load_points(i * n_rb)
            step((i - 1, n_rb - 1), (i, 0))

        def body(r, carry):
            load_points(i * n_rb + r)
            step((i, r - 1), (i, r))
            return carry

        lax.fori_loop(1, n_rb, body, 0)
    step((n_k - 1, n_rb - 1), None)
    if part == 0:
        t_ref[:, whole : whole + LANES] = lane_sum(src_ref, solutes, cols)


def add_tissue(t_ref, before_ref, sb, k_refs, first):
    rows = k_refs[0].shape[0]
    width = sb.shape[1]
    rb = min(1024, rows)
    pc = min(1024, width)
    for i, k_ref in enumerate(k_refs):
        for r in range(rows // rb):
            here = slice(i * rows + r * rb, i * rows + (r + 1) * rb)
            acc = None if before_ref is None else before_ref[:, here]
            for c in range(width // pc):
                got = lax.dot_general(
                    sb[:, c * pc : (c + 1) * pc],
                    k_ref[r * rb : (r + 1) * rb, pl.ds(first + c * pc, pc)],
                    (((1,), (1,)), ((), ())),
                    preferred_element_type=F32,
                )
                acc = got if acc is None else acc + got
            t_ref[:, here] = acc


def early_kernel(n_k, *refs):
    k_refs, refs = refs[:n_k], refs[n_k:]
    core_ref, mine_ref, t_ref, sb = refs
    half = mine_ref.shape[1]
    sb[...] = mine_ref[...].astype(BF16)
    add_tissue(t_ref, None, sb, k_refs, pl.multiple_of(core_ref[0] * half, half))


def tissue_kernel(part, n_k, *refs):
    k_refs, refs = refs[:n_k], refs[n_k:]
    solutes = refs[-1].shape[0]
    if part == 0:
        (
            core_ref, mine_ref, theirs_ref, cont_ref, flow_ref, early_ref, t_ref, src_ref, sb,
        ) = refs
        half = mine_ref.shape[1]
        sb[...] = theirs_ref[...].astype(BF16)
        other = pl.multiple_of((1 - core_ref[0]) * half, half)
        add_tissue(t_ref, early_ref, sb, k_refs, other)
        join_kernel(core_ref, mine_ref, theirs_ref, src_ref)
        whole = n_k * k_refs[0].shape[0]
        t_ref[:, whole + LANES :] = cont_ref[...] - src_ref[...] * flow_ref[...]
        t_ref[:, whole : whole + LANES] = lane_sum(src_ref, solutes, src_ref.shape[1])
    else:
        src_ref, t_ref, sb = refs
        sb[...] = src_ref[...].astype(BF16)
        add_tissue(t_ref, None, sb, k_refs, 0)


def join_kernel(core_ref, mine_ref, theirs_ref, src_ref):
    half = mine_ref.shape[1]
    core = core_ref[0]
    src_ref[:, at(core, half)] = mine_ref[...]
    src_ref[:, at(1 - core, half)] = theirs_ref[...]


def finish_kernel(
    core_ref, mine_ref, theirs_ref, cont_ref, level_a, level_b, level_ref, src_ref, cont_out
):
    rows = level_a.shape[1]
    join_kernel(core_ref, mine_ref, theirs_ref, src_ref)
    cont_out[...] = cont_ref[...]
    level_ref[:, 0:rows] = level_a[...]
    level_ref[:, rows : 2 * rows] = level_b[...]


def sinks(part, own_refs, got_refs, rates_ref, par_ref, base_ref, tmp, level_ref, first):
    whole = tmp.shape[1]
    solutes = rates_ref.shape[0]
    hs, dn, base = par_ref[0], par_ref[1], base_ref[...]
    total = jnp.zeros((solutes, LANES), F32)
    for p in range(0, whole, LANES):
        here = slice(p, p + LANES)
        level = base + (own_refs[:, here] + got_refs[:, here]) / dn
        rate = rates_ref[:, part * whole + p : part * whole + p + LANES]
        sink = rate * level / (jnp.abs(level) + hs)
        total = total + sink
        tmp[:, here] = sink.astype(BF16)
        if level_ref is not None:
            level_ref[:, first + p : first + p + LANES] = level
    return jnp.broadcast_to(jnp.sum(total, axis=1, keepdims=True), (solutes, LANES))


def add_wall(acc_ref, tmp, k_refs, first):
    width = acc_ref.shape[1] - LANES
    rows = k_refs[0].shape[0]
    for i, k_ref in enumerate(k_refs):
        acc_ref[:, 0:width] += jnp.dot(
            tmp[:, i * rows : (i + 1) * rows], k_ref[:, pl.ds(first, width)],
            preferred_element_type=F32,
        )


def wall_kernel(n_k, *refs):
    k_refs, refs = refs[:n_k], refs[n_k:]
    own_ref, got_ref, rates_ref, par_ref, base_ref, wall_ref, level_ref, tmp = refs
    solutes, cols = rates_ref.shape[0], k_refs[0].shape[1]
    total = sinks(0, own_ref, got_ref, rates_ref, par_ref, base_ref, tmp, level_ref, 0)
    wall_ref[:, 0:cols] = jnp.zeros((solutes, cols), F32)
    wall_ref[:, cols : cols + LANES] = total
    add_wall(wall_ref, tmp, k_refs, 0)


def send_kernel(last, n_k, *refs):
    k_refs, refs = refs[:n_k], refs[n_k:]
    (
        own_ref, got_ref, rates_ref, par_ref, base_ref, core_ref, before_ref,
        send_ref, tmp, *more,
    ) = refs
    cols = k_refs[0].shape[1]
    whole = tmp.shape[1]
    half = cols // 2
    level_ref = more[0] if last else None
    total = sinks(1, own_ref, got_ref, rates_ref, par_ref, base_ref, tmp, level_ref, 0)
    other = 1 - core_ref[0]
    send_ref[:, 0:half] = before_ref[:, at(other, half)]
    send_ref[:, half : half + LANES] = before_ref[:, cols : cols + LANES] + total
    add_wall(send_ref, tmp, k_refs, pl.multiple_of(other * half, half))


def keep_kernel(n_k, *refs):
    k_refs, refs = refs[:n_k], refs[n_k:]
    core_ref, before_ref, send_ref, tmp, keep_ref = refs
    half = k_refs[0].shape[1] // 2
    core = core_ref[0]
    keep_ref[:, 0:half] = before_ref[:, at(core, half)]
    keep_ref[:, half : half + LANES] = send_ref[:, half : half + LANES]
    add_wall(keep_ref, tmp, k_refs, pl.multiple_of(core * half, half))


def gather_kernel(ves_ref, parent_ref, got_ref, own_ref, inflow_ref, cont_ref, joined):
    solutes, cols = inflow_ref.shape
    start = own_ref.shape[1] - cols
    joined[:, 0:cols] = got_ref[:, start:]
    joined[:, cols : 2 * cols] = own_ref[:, start:]
    first = ves_ref[0] * cols
    tiles = cols // LANES

    def body(j, carry):
        here = at(j, LANES)
        parent = jnp.broadcast_to(parent_ref[0:1, here], (solutes, LANES))
        seg = first + j * LANES + lax.broadcasted_iota(jnp.int32, (solutes, LANES), 1)
        place = parent - (first - cols)
        lane = lax.bitwise_and(place, LANES - 1)
        tile = lax.shift_right_arithmetic(place, 7) - j
        acc = inflow_ref[:, here]
        tile = jnp.where(parent == seg, -1, tile)
        for t in range(tiles + 1):
            got = jnp.take_along_axis(joined[:, at(j + t, LANES)], lane, axis=1)
            acc = jnp.where(tile == t, got, acc)
        cont_ref[:, here] = acc
        return carry

    lax.fori_loop(0, tiles, body, 0)


def update_kernel(
    total_pts, total_segs, core_ref, a_ref, b_ref, own_ref, got_ref, src_ref, cont_ref, cond_ref,
    par_ref, base_ref, new_ref, *base_out
):
    half = new_ref.shape[1]
    rows = own_ref.shape[1] - src_ref.shape[1] - LANES
    core = core_ref[0]
    dp = par_ref[2]
    for p in range(half // LANES):
        here = slice(p * LANES, (p + 1) * LANES)
        there = at(core * (half // LANES) + p, LANES)
        wall = (a_ref[:, here] + b_ref[:, here]) / dp
        new_ref[:, here] = RELAX * src_ref[:, there] + RELAX * cond_ref[:, there] * (
            cont_ref[:, there] - wall
        )
    if base_out:
        sink_total = a_ref[:, half : half + LANES] + b_ref[:, half : half + LANES]
        source_total = own_ref[:, rows : rows + LANES] + got_ref[:, rows : rows + LANES]
        base_out[0][...] = base_ref[...] + BALANCE * (
            source_total / total_segs - sink_total / total_pts
        )


def body(
    point_xyz,
    point_cell,
    seg_xyz,
    seg_radius,
    conductance,
    flow_inv,
    parent,
    inflow,
    rate_table,
    half_sat,
    diffusivity,
    base_level,
    sources,
    contents,
):
    pts = point_xyz.shape[1]
    cols = seg_xyz.shape[1]
    solutes = sources.shape[0]
    n_tis = lax.axis_size("tis")
    n_ves = lax.axis_size("ves")
    total_pts = pts * n_tis
    total_segs = cols * n_ves
    rows = pts // PARTS
    half = cols // 2
    tis = lax.axis_index("tis")
    core = (tis % 2).astype(jnp.int32).reshape(1)
    ves = lax.axis_index("ves").astype(jnp.int32).reshape(1)

    def swap(value, bit):
        return lax.ppermute(value, "tis", [(i, i ^ bit) for i in range(n_tis)])

    def across(value):
        if n_ves == 2:
            return value, lax.ppermute(value, "ves", [(0, 1), (1, 0)])
        if value.shape[1] == rows:
            return lax.psum(value, "ves"), jnp.zeros_like(value)
        summed = lax.psum(value[:, : rows + LANES], "ves")
        tail = value[:, rows + LANES :]
        ahead = lax.ppermute(tail, "ves", [(i, (i + 1) % n_ves) for i in range(n_ves)])
        return (
            jnp.concatenate([summed, tail], axis=1),
            jnp.concatenate([jnp.zeros_like(summed), ahead], axis=1),
        )

    cond = conductance.reshape(1, cols)
    flow = flow_inv.reshape(1, cols)
    par_row = parent.reshape(1, cols)

    chunk = rows // CHUNKS
    pieces = [[None] * CHUNKS for _ in range(PARTS)]
    level = None
    for sweep in range(ITERS):
        last = sweep == ITERS - 1
        own, got = [], []
        for part in range(PARTS):
            if sweep == 0:
                ins = [
                    ("h", point_xyz), ("h", seg_xyz), ("h", seg_radius.reshape(1, cols)),
                    ("h", sources),
                ]
                outs = [pltpu.VMEM((chunk, cols), BF16)] * CHUNKS + [
                    shape(solutes, rows + (LANES + cols if part == 0 else 0))
                ]
                if part == 0:
                    ins = [("s", core), ("s", ves)] + ins + [
                        ("h", rate_table), ("h", point_cell.reshape(1, pts)), ("hs", half_sat),
                        ("hs", diffusivity), ("hs", base_level), ("h", contents), ("h", flow),
                    ]
                    outs += [
                        shape(solutes, pts), shape(3, solutes, LANES), shape(solutes, LANES),
                    ]
                else:
                    ins += [("v", t)]
                *made, = call(
                    functools.partial(
                        build_kernel, part, float(total_pts), float(total_segs), CHUNKS
                    ),
                    outs,
                    ins,
                    f"build{part}",
                    scratch=[
                        pltpu.VMEM((3, min(BUILD_ROWS, chunk), LANES), F32),
                        pltpu.VMEM((1, cols), F32), pltpu.VMEM((solutes, cols), BF16),
                    ],
                    limit=BUILD_LIMIT,
                    flops=10 * rows * cols,
                    bytes_accessed=40_000_000,
                )
                pieces[part], t, more = made[:CHUNKS], made[CHUNKS], made[CHUNKS + 1 :]
                if part == 0:
                    rates, par, base = more
            else:
                outs = [shape(solutes, rows + (LANES + cols if part == 0 else 0))]
                ins = [("k", piece) for piece in pieces[part]]
                if part == 0:
                    outs += [shape(solutes, cols)]
                    ins += [
                        ("s", core), ("v", new), ("v", theirs), ("v", contents), ("v", flow),
                        ("v", early),
                    ]
                else:
                    ins += [("v", sources)]
                t, *more = call(
                    functools.partial(tissue_kernel, part, CHUNKS),
                    outs,
                    ins,
                    f"tissue{part}",
                    limit=18,
                    scratch=[pltpu.VMEM((solutes, half if part == 0 else cols), BF16)],
                    flops=2 * solutes * rows * cols,
                    bytes_accessed=10_000_000,
                )
                if part == 0:
                    (sources,) = more
            mine, other = across(t)
            own.append(mine)
            got.append(other)

        def wall_ins(part):
            return [("k", piece) for piece in pieces[part]] + [
                ("v", own[part]), ("v", got[part]), ("v", rates), ("v", par), ("v", base),
            ]

        wall, level = call(
            functools.partial(wall_kernel, CHUNKS),
            [shape(solutes, cols + LANES), shape(solutes, rows)],
            wall_ins(0),
            "wall0",
            limit=18,
            scratch=[pltpu.VMEM((solutes, rows), BF16)],
            flops=2 * solutes * rows * cols,
            bytes_accessed=10_000_000,
        )
        send, sink, *more = call(
            functools.partial(send_kernel, last, CHUNKS),
            [shape(solutes, half + LANES), jax.ShapeDtypeStruct((solutes, rows), BF16)]
            + ([shape(solutes, rows)] if last else []),
            wall_ins(1) + [("s", core), ("v", wall)],
            "send",
            limit=18,
            flops=solutes * rows * cols,
            bytes_accessed=5_000_000,
        )
        theirs = swap(send, 1)
        (keep,) = call(
            functools.partial(keep_kernel, CHUNKS),
            [shape(solutes, half + LANES)],
            [("k", piece) for piece in pieces[1]]
            + [("s", core), ("v", wall), ("v", send), ("v", sink)],
            "keep",
            limit=18,
            flops=solutes * rows * cols,
            bytes_accessed=5_000_000,
        )
        if last:
            levels = (level, more[0])
        (new_contents,) = call(
            gather_kernel,
            [shape(solutes, cols)],
            [("s", ves), ("v", par_row), ("v", got[0]), ("v", own[0]), ("v", inflow)],
            "gather",
            scratch=[pltpu.VMEM((solutes, 2 * cols), F32)],
            flops=solutes * cols * 33,
            bytes_accessed=8_000_000,
        )
        bit = 2
        while bit < n_tis:
            keep = keep + theirs
            theirs = swap(keep, bit)
            bit *= 2
        new, *rest = call(
            functools.partial(update_kernel, float(total_pts), float(total_segs)),
            [shape(solutes, half)] + ([] if last else [shape(solutes, LANES)]),
            [
                ("s", core), ("v", keep), ("v", theirs), ("v", own[0]), ("v", got[0]),
                ("v", sources), ("v", new_contents), ("v", cond), ("v", par), ("v", base),
            ],
            "update",
        )
        base = base if last else rest[0]
        contents = new_contents
        theirs = swap(new, 1)
        if not last:
            (early,) = call(
                functools.partial(early_kernel, CHUNKS),
                [shape(solutes, rows)],
                [("k", piece) for piece in pieces[0]] + [("s", core), ("v", new)],
                "early",
                limit=18,
                scratch=[pltpu.VMEM((solutes, half), BF16)],
                flops=solutes * rows * cols,
                bytes_accessed=5_000_000,
            )
    return call(
        finish_kernel,
        [shape(solutes, pts), shape(solutes, cols), shape(solutes, cols)],
        [("s", core), ("v", new), ("v", theirs), ("v", contents)] + [("v", x) for x in levels],
        "finish",
    )


def solution(mesh):
    return jax.shard_map(
        body,
        mesh=mesh,
        in_specs=(
            P(None, "tis"),
            P("tis"),
            P(None, "ves"),
            P("ves"),
            P("ves"),
            P("ves"),
            P("ves"),
            P(None, "ves"),
            P(),
            P(),
            P(),
            P(),
            P(None, "ves"),
            P(None, "ves"),
        ),
        out_specs=(P(None, "tis"), P(None, "ves"), P(None, "ves")),
        check_vma=False,
    )
```
